128 devices in a mesh: src: 16 (over x, z_lo, core), freq: 8 (over y, z_hi).
Axes of the slice: x: 4, y: 4, z: 4 (z_hi: 2, z_lo: 2; z = z_hi * 2 + z_lo), core: 2. Of those that a mesh axis runs over, the one named last changes fastest.
Arguments:
- receivers: bfloat16 [8, 16, 2, 256, 512], P('freq', 'src'), may hold values from -6 to 6
- data: bfloat16 [8, 2, 8192, 2048], P('freq', None, None, 'src'), may hold values from -0.046875 to 0.046875
- block_of_slot: int32 [16], replicated, may hold values from 0 to 15, each once
- receiver_order: int32 [256], replicated, may hold values from 0 to 255, each once
Outputs:
- traces: bfloat16 [256, 2048, 256], P('freq', 'src')
The draws below stay inside these ranges and needn't reach their ends.
Inputs may be any that keep to these rules, and one draw needn't show every extreme that they name: `block_of_slot`: each of the 16 bounce blocks is held in exactly one slot. `receiver_order`: each receiver appears in exactly one trace row.
All inputs are finite; a program needn't handle non-finite values.
Results may differ from the reference program's by a relative error of at most 0.0049.
Values may be sent and summed in bfloat16 or wider, within the bound.
A program may use at most 64 MiB of HBM per device.

```python
import math
import jax
import jax.numpy as jnp
from jax import lax

R = 256
KB = 512
NT = 256
NB = 16
K = 8192
S = 2048
F = 8


def block_scale(stream_key, shape, cuts, low, high):
    level, own = 1.0, jax.random.fold_in(stream_key, 6)
    for axis_at, blocks in cuts:
        draws = jnp.exp(jax.random.uniform(jax.random.fold_in(own, axis_at), (blocks,), jnp.float32, low / len(cuts), high / len(cuts)))
        level = level * jnp.repeat(draws, shape[axis_at] // blocks).reshape([-1 if axis == axis_at else 1 for axis in range(len(shape))])
    return level


def gaussian(own_key, shape, scale, bound, shards=(), kind=jnp.bfloat16):
    array = scale * jax.random.normal(own_key, shape, jnp.float32)
    if shards:
        array = array * block_scale(own_key, shape, shards, -0.22, 0.18)
    return jnp.clip(array, -bound, bound).astype(kind)


def setup_inputs(seed: int = 0) -> dict:
    key_list = jax.random.split(jax.random.key(seed), 5)
    return {
        "receivers": gaussian(key_list[0], (F, NB, 2, R, KB), 1.0, 6.0, ((0, 8), (1, 16))),
        "data": gaussian(key_list[1], (F, 2, K, S), (2 * K) ** -0.5, 0.046875, ((0, 8), (3, 16))),
        "block_of_slot": jax.random.permutation(key_list[2], NB).astype(jnp.int32),
        "receiver_order": jax.random.permutation(key_list[3], R).astype(jnp.int32),
    }


def reference(receivers, data, block_of_slot, receiver_order):
    high = lax.Precision.HIGHEST

    def turn(acc, slot):
        block = block_of_slot[slot]
        rows = lax.dynamic_slice_in_dim(data, (block * KB).astype(jnp.int32), KB, 2).astype(jnp.float32)
        piece = lax.dynamic_index_in_dim(receivers, slot, 1, keepdims=False).astype(jnp.float32)
        g_re, g_im = piece[:, 0], piece[:, 1]
        d_re, d_im = rows[:, 0], rows[:, 1]
        real = jnp.einsum('frk,fks->frs', g_re, d_re, precision=high) - jnp.einsum('frk,fks->frs', g_im, d_im, precision=high)
        imag = jnp.einsum('frk,fks->frs', g_re, d_im, precision=high) + jnp.einsum('frk,fks->frs', g_im, d_re, precision=high)
        return acc + jnp.stack([real, imag], 1), None

    start = jnp.zeros((F, 2, R, S), jnp.float32)
    acc, _ = lax.scan(turn, start, jnp.arange(NB, dtype=jnp.int32))
    spectra = acc.astype(jnp.bfloat16)
    ordered = jnp.take(spectra, receiver_order, axis=2).astype(jnp.float32)
    times = jnp.arange(NT, dtype=jnp.int32)
    bins = (2 * jnp.arange(F, dtype=jnp.int32) + 1) * (NT // (4 * F))
    phase = (bins[:, None] * times[None, :]) % NT
    angle = phase.astype(jnp.float32) * (2.0 * math.pi / NT)
    cosine = jnp.cos(angle)
    sine = jnp.sin(angle)
    scale = F ** -0.5

    def one_row(row):
        real = ordered[:, 0, row, :]
        imag = ordered[:, 1, row, :]
        value = jnp.einsum('fs,ft->st', real, cosine, precision=high) - jnp.einsum('fs,ft->st', imag, sine, precision=high)
        return (value * scale).astype(jnp.bfloat16)

    return lax.map(one_row, jnp.arange(R, dtype=jnp.int32))
```

```python
import math

import jax
import jax.numpy as jnp
import numpy as np
from jax import lax
from jax.sharding import PartitionSpec as P

NT = 256


def tables(count):
    times = np.arange(NT)
    bins = (2 * np.arange(count) + 1) * (NT // (4 * count))
    angle = (bins[:, None] * times[None, :] % NT) * (2.0 * math.pi / NT)
    full = np.stack([np.cos(angle), -np.sin(angle)], 1) * count ** (-0.5)
    return full.astype(np.float32)


def body(receivers, data, block_of_slot, receiver_order):
    width = receivers.shape[4]
    blocks = lax.all_gather(receivers[0], "src", axis=0, tiled=True)
    slots = blocks.shape[0]
    rows = data[0].reshape(2, slots, width, data.shape[3])
    slot_of_block = jnp.argsort(block_of_slot)
    moved = jnp.take(blocks, slot_of_block, axis=0)
    acc = jnp.einsum("jcrk,djks->cdrs", moved, rows, preferred_element_type=jnp.float32)
    spectra = jnp.stack([acc[0, 0] - acc[1, 1], acc[0, 1] + acc[1, 0]], 0).astype(jnp.bfloat16)
    ordered = jnp.take(spectra, receiver_order, axis=1)[None]
    got = lax.all_to_all(ordered, "freq", split_axis=2, concat_axis=0, tiled=True)
    table = jnp.asarray(tables(got.shape[0]))
    high = table.astype(jnp.bfloat16)
    low = (table - high.astype(jnp.float32)).astype(jnp.bfloat16)
    value = jnp.einsum("fcrs,fct->rst", got, high, preferred_element_type=jnp.float32)
    value = value + jnp.einsum("fcrs,fct->rst", got, low, preferred_element_type=jnp.float32)
    return value.astype(jnp.bfloat16)


def solution(mesh):
    placed = (P("freq", "src", None, None, None), P("freq", None, None, "src"), P(), P())
    return jax.shard_map(
        body, mesh=mesh, in_specs=placed, out_specs=P("freq", "src", None), check_vma=False
    )
```

```python
import functools
import math

import jax
import jax.numpy as jnp
import numpy as np
from jax import lax
from jax.experimental import pallas as pl
from jax.experimental.pallas import tpu as pltpu
from jax.sharding import PartitionSpec as P

NT = 256
MESH = pl.DeviceIdType.MESH
CHUNK = 64

SENDS = {
    "xp": [(0, 0, 0, 4), (0, 0, 4, 4)]
    + [(-1, 0, k, 1) for k in range(4)]
    + [(0, 1, 1, 3), (0, 1, 4, 2), (0, 1, 6, 2)],
    "xm": [(0, 0, 4, 4), (0, 0, 0, 4)]
    + [(1, 0, 4 + k, 1) for k in range(4)]
    + [(0, 1, 4, 3), (0, 1, 2, 2), (0, 1, 0, 2)],
    "z": [(0, 0, 0, 4), (0, 0, 4, 4), (-1, 0, 0, 1), (1, 0, 7, 1)]
    + [(2, 0, 4 * (k % 2) + k // 2, 1) for k in range(8)],
    "c": [(0, 0, 0, 4), (0, 0, 4, 4)]
    + [(-1, 0, 0, 4), (1, 0, 4, 4), (0, 1, 0, 4)]
    + [(-1, 0, 4, 4), (1, 0, 0, 4), (0, 1, 4, 4)]
    + [(2, 0, 0, 4), (2, 0, 4, 4)]
    + [(-1, 1, 0, 4), (1, 1, 4, 4), (2, 1, 0, 2), (2, 1, 4, 2)]
    + [(-1, 1, 4, 2), (1, 1, 2, 2)]
    + [(2, 1, 2, 2), (2, 1, 6, 2)]
    + [(-1, 1, 6, 2), (1, 1, 0, 2)],
}
SHIFT = {"xp": (-1, 0, 0), "xm": (1, 0, 0), "z": (0, 1, 0), "c": (0, 0, 1)}
COUNT = {link: len(rows) for link, rows in SENDS.items()}


def tables(count):
    times = np.arange(NT)
    bins = (2 * np.arange(count) + 1) * (NT // (4 * count))
    angle = (bins[:, None] * times[None, :] % NT) * (2.0 * math.pi / NT)
    full = np.stack([np.cos(angle), -np.sin(angle)], 1) * count ** (-0.5)
    full = full.reshape(2 * count, NT).astype(np.float32)
    high = full.astype(jnp.bfloat16).astype(np.float32)
    low = (full - high).astype(jnp.bfloat16).astype(np.float32)
    return np.concatenate([high, low], 0)


def gather_kernel(
    freqs, block_ref, order_ref, own_hbm, data_hbm, out_ref,
    held, data, acc, perm, mix, outgoing, arrived,
    sx, rx, sf, rf, local,
):
    me = lax.axis_index("src")
    mine = lax.axis_index("freq")
    x, z, c = me // 4, (me // 2) % 2, me % 2
    depth = own_hbm.shape[1]
    rows = own_hbm.shape[0] // 2
    part = rows // freqs

    def slot(dx, dz, dc):
        return ((x + dx + 4) % 4) * 4 + ((z + dz) % 2) * 2 + (c + dc) % 2

    target = {"xp": slot(1, 0, 0), "xm": slot(-1, 0, 0), "z": slot(0, 1, 0), "c": slot(0, 0, 1)}
    first = {}
    at = 0
    for link in SENDS:
        first[link] = at
        at += COUNT[link]

    own_copy = pltpu.make_async_copy(own_hbm, held.at[me], local.at[0])
    data_copy = pltpu.make_async_copy(data_hbm, data, local.at[1])
    own_copy.start()
    data_copy.start()

    barrier = pltpu.get_barrier_semaphore()
    for link in SENDS:
        pl.semaphore_signal(barrier, inc=1, device_id={"src": target[link]}, device_id_type=MESH)
    for d in range(1, freqs):
        pl.semaphore_signal(barrier, inc=1, device_id={"freq": (mine + d) % freqs}, device_id_type=MESH)
    pl.semaphore_wait(barrier, len(SENDS) + freqs - 1)

    def copy(link, k, received=False):
        dx, dz, low, count = SENDS[link][k]
        dc = 0
        if received:
            sx_, sz_, dc = SHIFT[link]
            dx, dz = dx + sx_, dz + sz_
        piece = held.at[slot(dx, dz, dc), pl.ds(low * CHUNK, count * CHUNK)]
        return pltpu.make_async_remote_copy(
            src_ref=piece,
            dst_ref=piece,
            send_sem=sx.at[first[link] + k],
            recv_sem=rx.at[first[link] + k],
            device_id={"src": target[link]},
            device_id_type=MESH,
        )

    def send(link, *which):
        for k in which:
            copy(link, k).start()

    def wait(link, *which):
        for k in which:
            copy(link, k, True).wait_recv()

    def product(dx, dz, dc, low, count, fresh=False):
        j = slot(dx, dz, dc)
        block = block_ref[j]
        right = jnp.concatenate([data[0, block], data[1, block]], 1)
        span = pl.ds(low * CHUNK, count * CHUNK)
        value = jnp.dot(held[j, span, :], right, preferred_element_type=jnp.float32)
        if fresh:
            acc[span, :] = value
        else:
            acc[span, :] += value

    own_copy.wait()
    send("xp", 0)
    send("xm", 0)
    send("z", 0)
    send("xp", 1)
    send("xm", 1)
    send("z", 1)
    send("c", 0, 1)

    ids = lax.broadcasted_iota(jnp.int32, (rows, rows), 0)
    chosen = jnp.where(ids == order_ref[...], 1.0, 0.0).astype(jnp.float32)
    perm[...] = chosen.T.astype(jnp.bfloat16)
    n = lax.broadcasted_iota(jnp.int32, (2 * rows, 1), 0)
    source = (n % 2) * rows + ((n // 2) % freqs) * part + n // (2 * freqs)
    m = lax.broadcasted_iota(jnp.int32, (2 * rows, 2 * rows), 1)
    mix[...] = jnp.where(m == source, 1.0, 0.0).astype(jnp.bfloat16)

    data_copy.wait()
    product(0, 0, 0, 0, 8, fresh=True)
    wait("c", 0, 1)
    product(0, 0, 1, 0, 8)

    wait("xp", 0)
    send("xp", 2, 3, 4, 5)
    send("z", 2)
    send("c", 2)
    wait("xm", 0)
    send("xm", 2, 3, 4, 5)
    send("z", 3)
    send("c", 3)
    wait("z", 0)
    send("c", 4)
    product(-1, 0, 0, 0, 4)
    product(1, 0, 0, 4, 4)
    product(0, 1, 0, 0, 4)
    wait("c", 2, 3, 4)
    product(-1, 0, 1, 0, 4)
    product(1, 0, 1, 4, 4)
    product(0, 1, 1, 0, 4)

    wait("z", 1)
    send("xp", 6, 7, 8)
    send("xm", 6, 7, 8)
    wait("xp", 1)
    send("c", 5)
    wait("xm", 1)
    send("c", 6, 7)
    product(-1, 0, 0, 4, 4)
    product(1, 0, 0, 0, 4)
    product(0, 1, 0, 4, 4)
    wait("c", 5, 6, 7)
    product(-1, 0, 1, 4, 4)
    product(1, 0, 1, 0, 4)
    product(0, 1, 1, 4, 4)

    for k in range(4):
        wait("xp", 2 + k)
        send("z", 4 + 2 * k)
        wait("xm", 2 + k)
        send("z", 5 + 2 * k)
    send("c", 8, 9)
    product(2, 0, 0, 0, 8)
    wait("c", 8, 9)
    product(2, 0, 1, 0, 8)

    wait("z", 2, 3)
    wait("xp", 6)
    send("c", 10)
    wait("xm", 6)
    send("c", 11)
    wait("z", 4, 5, 6, 7)
    send("c", 12, 13)
    product(-1, 1, 0, 0, 4)
    product(1, 1, 0, 4, 4)
    wait("c", 10, 11)
    product(-1, 1, 1, 0, 4)
    product(1, 1, 1, 4, 4)

    wait("xp", 7)
    send("c", 14)
    wait("xm", 7)
    send("c", 15)
    product(-1, 1, 0, 4, 2)
    product(1, 1, 0, 2, 2)
    wait("z", 8, 10)
    send("c", 16)
    wait("z", 9, 11)
    send("c", 17)
    product(2, 1, 0, 0, 8)
    wait("c", 14, 15)
    product(-1, 1, 1, 4, 2)
    product(1, 1, 1, 2, 2)
    wait("c", 12, 13, 16, 17)
    product(2, 1, 1, 0, 8)

    wait("xp", 8)
    send("c", 18)
    wait("xm", 8)
    send("c", 19)
    product(-1, 1, 0, 6, 2)
    product(1, 1, 0, 0, 2)
    wait("c", 18, 19)
    product(-1, 1, 1, 6, 2)
    product(1, 1, 1, 0, 2)

    half = acc.shape[1] // 2
    real = acc[:rows, :half] - acc[rows:, half:]
    imag = acc[:rows, half:] + acc[rows:, :half]
    spectra = jnp.concatenate([real, imag], 1).astype(jnp.bfloat16)
    outgoing[...] = jnp.dot(perm[...], spectra, preferred_element_type=jnp.float32).astype(jnp.bfloat16)

    def share(d, received=False):
        peer = (mine + d) % freqs
        back = (mine - d + freqs) % freqs
        taken = outgoing.at[pl.ds(pl.multiple_of(peer * part, part), part)]
        landing = back if received else mine
        return pltpu.make_async_remote_copy(
            src_ref=taken,
            dst_ref=arrived.at[pl.ds(pl.multiple_of(landing * part, part), part)],
            send_sem=sf.at[d],
            recv_sem=rf.at[d],
            device_id={"freq": peer},
            device_id_type=MESH,
        )

    for d in range(1, freqs):
        share(d).start()
    here = pl.ds(pl.multiple_of(mine * part, part), part)
    keep = pltpu.make_async_copy(outgoing.at[here], arrived.at[here], local.at[0])
    keep.start()
    for link in SENDS:
        for k in range(COUNT[link]):
            copy(link, k).wait_send()
    keep.wait()
    for d in range(1, freqs):
        share(d, True).wait_recv()

    stacked = jnp.concatenate([arrived[:, :half], arrived[:, half:]], 0)
    mixed = jnp.dot(mix[...], stacked, preferred_element_type=jnp.float32)
    for g in range(2 * rows // half):
        span = pl.ds(g * half, half)
        out_ref[span, :] = mixed[g * half : (g + 1) * half, :].T.astype(jnp.bfloat16)
    for d in range(1, freqs):
        share(d).wait_send()


def transform_kernel(spectra_ref, table_ref, out_ref):
    step = pl.program_id(0)
    coefs = table_ref.shape[0] // 2
    each = spectra_ref.shape[1] // coefs
    high, low = table_ref[:coefs, :], table_ref[coefs:, :]
    full = jnp.concatenate([high] * each + [low] * each, 0)
    row = lax.broadcasted_iota(jnp.int32, full.shape, 0)
    right = jnp.where((row // coefs) % each == step, full, 0.0).astype(jnp.bfloat16)
    left = jnp.concatenate([spectra_ref[...], spectra_ref[...]], 1)
    value = jnp.dot(left, right, preferred_element_type=jnp.float32)
    out_ref[...] = value.astype(jnp.bfloat16).reshape(out_ref.shape)


def body(freqs, receivers, data, block_of_slot, receiver_order):
    rows, depth = receivers.shape[3], receivers.shape[4]
    points, width = data.shape[2], data.shape[3]
    slots = block_of_slot.shape[0]
    part = rows // freqs
    copies = sum(COUNT.values())
    moved = pl.pallas_call(
        functools.partial(gather_kernel, freqs),
        out_shape=jax.ShapeDtypeStruct((2 * rows, width), jnp.bfloat16),
        in_specs=[
            pl.BlockSpec(memory_space=pltpu.SMEM),
            pl.BlockSpec(memory_space=pltpu.VMEM),
            pl.BlockSpec(memory_space=pl.ANY),
            pl.BlockSpec(memory_space=pl.ANY),
        ],
        out_specs=pl.BlockSpec(memory_space=pltpu.VMEM),
        scratch_shapes=[
            pltpu.VMEM((slots, 2 * rows, depth), jnp.bfloat16),
            pltpu.VMEM((2, slots, depth, width), jnp.bfloat16),
            pltpu.VMEM((2 * rows, 2 * width), jnp.float32),
            pltpu.VMEM((rows, rows), jnp.bfloat16),
            pltpu.VMEM((2 * rows, 2 * rows), jnp.bfloat16),
            pltpu.VMEM((rows, 2 * width), jnp.bfloat16),
            pltpu.VMEM((rows, 2 * width), jnp.bfloat16),
            pltpu.SemaphoreType.DMA((copies,)),
            pltpu.SemaphoreType.DMA((copies,)),
            pltpu.SemaphoreType.DMA((freqs,)),
            pltpu.SemaphoreType.DMA((freqs,)),
            pltpu.SemaphoreType.DMA((2,)),
        ],
        compiler_params=pltpu.CompilerParams(
            collective_id=0, has_side_effects=True, vmem_limit_bytes=60 * 2**20
        ),
        name="gather_multiply_exchange",
    )(
        block_of_slot,
        receiver_order.reshape(1, rows),
        receivers.reshape(2 * rows, depth),
        data.reshape(2, slots, points // slots, width),
    )
    table = jnp.asarray(tables(freqs))
    each = width // (2 * freqs)
    groups = part // each
    traces = pl.pallas_call(
        transform_kernel,
        out_shape=jax.ShapeDtypeStruct((groups, each, width, NT), jnp.bfloat16),
        grid=(each,),
        in_specs=[
            pl.BlockSpec(moved.shape, lambda i: (0, 0)),
            pl.BlockSpec(table.shape, lambda i: (0, 0)),
        ],
        out_specs=pl.BlockSpec((groups, 1, width, NT), lambda i: (0, i, 0, 0)),
        name="transform",
    )(moved, table)
    return traces.reshape(part, width, NT)


def solution(mesh):
    placed = (P("freq", "src", None, None, None), P("freq", None, None, "src"), P(), P())
    return jax.shard_map(
        functools.partial(body, mesh.shape["freq"]),
        mesh=mesh,
        in_specs=placed,
        out_specs=P("freq", "src", None),
        check_vma=False,
    )
```

```python
import functools
import math

import jax
import jax.numpy as jnp
import numpy as np
from jax import lax
from jax.experimental import pallas as pl
from jax.experimental.pallas import tpu as pltpu
from jax.sharding import PartitionSpec as P

NT = 256
MESH = pl.DeviceIdType.MESH
CHUNK = 64

SENDS = {
    "xp": [(0, 0, 0, 4), (0, 0, 4, 4)]
    + [(-1, 0, k, 1) for k in range(4)]
    + [(0, 1, 1, 3), (0, 1, 4, 2), (0, 1, 6, 2)],
    "xm": [(0, 0, 4, 4), (0, 0, 0, 4)]
    + [(1, 0, 4 + k, 1) for k in range(4)]
    + [(0, 1, 4, 3), (0, 1, 2, 2), (0, 1, 0, 2)],
    "z": [(0, 0, 0, 4), (0, 0, 4, 4), (-1, 0, 0, 1), (1, 0, 7, 1)]
    + [(2, 0, 4 * (k % 2) + k // 2, 1) for k in range(8)],
    "c": [(0, 0, 0, 4), (0, 0, 4, 4)]
    + [(-1, 0, 0, 4), (1, 0, 4, 4), (0, 1, 0, 4)]
    + [(-1, 0, 4, 4), (1, 0, 0, 4), (0, 1, 4, 4)]
    + [(2, 0, 0, 4), (2, 0, 4, 4)]
    + [(-1, 1, 0, 4), (1, 1, 4, 4), (2, 1, 0, 2), (2, 1, 4, 2)]
    + [(-1, 1, 4, 2), (1, 1, 2, 2)]
    + [(2, 1, 2, 2), (2, 1, 6, 2)]
    + [(-1, 1, 6, 2), (1, 1, 0, 2)],
}
SHIFT = {"xp": (-1, 0, 0), "xm": (1, 0, 0), "z": (0, 1, 0), "c": (0, 0, 1)}
COUNT = {link: len(rows) for link, rows in SENDS.items()}


def tables(count):
    times = np.arange(NT)
    bins = (2 * np.arange(count) + 1) * (NT // (4 * count))
    angle = (bins[:, None] * times[None, :] % NT) * (2.0 * math.pi / NT)
    full = np.stack([np.cos(angle), -np.sin(angle)], 1) * count ** (-0.5)
    full = full.reshape(2 * count, NT).astype(np.float32)
    high = full.astype(jnp.bfloat16).astype(np.float32)
    low = (full - high).astype(jnp.bfloat16).astype(np.float32)
    return np.concatenate([high, low], 0)


def gather_kernel(
    freqs, block_ref, order_ref, own_hbm, data_hbm, out_ref,
    held, data, acc, perm, mix, outgoing, arrived,
    sx, rx, sf, rf, local, known,
):
    me = lax.axis_index("src")
    mine = lax.axis_index("freq")
    x, z, c = me // 4, (me // 2) % 2, me % 2
    depth = own_hbm.shape[1]
    rows = own_hbm.shape[0] // 2
    part = rows // freqs

    def slot(dx, dz, dc):
        return ((x + dx + 4) % 4) * 4 + ((z + dz) % 2) * 2 + (c + dc) % 2

    target = {"xp": slot(1, 0, 0), "xm": slot(-1, 0, 0), "z": slot(0, 1, 0), "c": slot(0, 0, 1)}
    first = {}
    at = 0
    for link in SENDS:
        first[link] = at
        at += COUNT[link]

    own_copy = pltpu.make_async_copy(own_hbm, held.at[me], local.at[0])
    data_copy = pltpu.make_async_copy(data_hbm, data, local.at[1])
    own_copy.start()
    data_copy.start()

    barrier = pltpu.get_barrier_semaphore()
    for link in SENDS:
        pl.semaphore_signal(barrier, inc=1, device_id={"src": target[link]}, device_id_type=MESH)
    after, before = {"freq": (mine + 2) % freqs}, {"freq": (mine + freqs - 2) % freqs}
    inner, outer = {"src": target["z"]}, {"src": target["z"], "freq": mine + 1 - 2 * (mine % 2)}
    for peer in (after, before, outer):
        pl.semaphore_signal(barrier, inc=1, device_id=peer, device_id_type=MESH)
    pl.semaphore_wait(barrier, len(SENDS) + 3)

    rounds = ((before, inner), (before, after), (before,))

    def tell(k):
        for peer in rounds[k]:
            pl.semaphore_signal(known.at[k], inc=1, device_id=peer, device_id_type=MESH)

    def hear(k):
        pl.semaphore_wait(known.at[k], len(rounds[k]))

    def copy(link, k, received=False):
        dx, dz, low, count = SENDS[link][k]
        dc = 0
        if received:
            sx_, sz_, dc = SHIFT[link]
            dx, dz = dx + sx_, dz + sz_
        piece = held.at[slot(dx, dz, dc), pl.ds(low * CHUNK, count * CHUNK)]
        return pltpu.make_async_remote_copy(
            src_ref=piece,
            dst_ref=piece,
            send_sem=sx.at[first[link] + k],
            recv_sem=rx.at[first[link] + k],
            device_id={"src": target[link]},
            device_id_type=MESH,
        )

    def send(link, *which):
        for k in which:
            copy(link, k).start()

    def wait(link, *which):
        for k in which:
            copy(link, k, True).wait_recv()

    def product(dx, dz, dc, low, count, fresh=False):
        j = slot(dx, dz, dc)
        block = block_ref[j]
        right = jnp.concatenate([data[0, block], data[1, block]], 1)
        span = pl.ds(low * CHUNK, count * CHUNK)
        value = jnp.dot(held[j, span, :], right, preferred_element_type=jnp.float32)
        if fresh:
            acc[span, :] = value
        else:
            acc[span, :] += value

    own_copy.wait()
    send("xp", 0)
    send("xm", 0)
    send("z", 0)
    send("xp", 1)
    send("xm", 1)
    send("z", 1)
    send("c", 0, 1)
    tell(0)

    ids = lax.broadcasted_iota(jnp.int32, (rows, rows), 0)
    chosen = jnp.where(ids == order_ref[...], 1.0, 0.0).astype(jnp.float32)
    perm[...] = chosen.T.astype(jnp.bfloat16)
    n = lax.broadcasted_iota(jnp.int32, (2 * rows, 1), 0)
    source = (n % 2) * rows + ((n // 2) % freqs) * part + n // (2 * freqs)
    m = lax.broadcasted_iota(jnp.int32, (2 * rows, 2 * rows), 1)
    mix[...] = jnp.where(m == source, 1.0, 0.0).astype(jnp.bfloat16)

    data_copy.wait()
    product(0, 0, 0, 0, 8, fresh=True)
    wait("c", 0, 1)
    product(0, 0, 1, 0, 8)

    wait("xp", 0)
    send("xp", 2, 3, 4, 5)
    send("z", 2)
    send("c", 2)
    wait("xm", 0)
    send("xm", 2, 3, 4, 5)
    send("z", 3)
    send("c", 3)
    wait("z", 0)
    send("c", 4)
    product(-1, 0, 0, 0, 4)
    product(1, 0, 0, 4, 4)
    product(0, 1, 0, 0, 4)
    hear(0)
    tell(1)
    wait("c", 2, 3, 4)
    product(-1, 0, 1, 0, 4)
    product(1, 0, 1, 4, 4)
    product(0, 1, 1, 0, 4)

    wait("z", 1)
    send("xp", 6, 7, 8)
    send("xm", 6, 7, 8)
    wait("xp", 1)
    send("c", 5)
    wait("xm", 1)
    send("c", 6, 7)
    product(-1, 0, 0, 4, 4)
    product(1, 0, 0, 0, 4)
    product(0, 1, 0, 4, 4)
    hear(1)
    tell(2)
    wait("c", 5, 6, 7)
    hear(2)
    product(-1, 0, 1, 4, 4)
    product(1, 0, 1, 0, 4)
    product(0, 1, 1, 4, 4)

    for k in range(4):
        wait("xp", 2 + k)
        send("z", 4 + 2 * k)
        wait("xm", 2 + k)
        send("z", 5 + 2 * k)
    send("c", 8, 9)
    product(2, 0, 0, 0, 8)
    wait("c", 8, 9)
    product(2, 0, 1, 0, 8)

    wait("z", 2, 3)
    wait("xp", 6)
    send("c", 10)
    wait("xm", 6)
    send("c", 11)
    wait("z", 4, 5, 6, 7)
    send("c", 12, 13)
    product(-1, 1, 0, 0, 4)
    product(1, 1, 0, 4, 4)
    wait("c", 10, 11)
    product(-1, 1, 1, 0, 4)
    product(1, 1, 1, 4, 4)

    wait("xp", 7)
    send("c", 14)
    wait("xm", 7)
    send("c", 15)
    product(-1, 1, 0, 4, 2)
    product(1, 1, 0, 2, 2)
    wait("z", 8, 10)
    send("c", 16)
    wait("z", 9, 11)
    send("c", 17)
    product(2, 1, 0, 0, 8)
    wait("c", 14, 15)
    product(-1, 1, 1, 4, 2)
    product(1, 1, 1, 2, 2)
    wait("c", 12, 13, 16, 17)
    product(2, 1, 1, 0, 8)

    wait("xp", 8)
    send("c", 18)
    wait("xm", 8)
    send("c", 19)
    product(-1, 1, 0, 6, 2)
    product(1, 1, 0, 0, 2)
    wait("c", 18, 19)
    product(-1, 1, 1, 6, 2)
    product(1, 1, 1, 0, 2)

    half = acc.shape[1] // 2
    real = acc[:rows, :half] - acc[rows:, half:]
    imag = acc[:rows, half:] + acc[rows:, :half]
    spectra = jnp.concatenate([real, imag], 1).astype(jnp.bfloat16)
    outgoing[...] = jnp.dot(perm[...], spectra, preferred_element_type=jnp.float32).astype(jnp.bfloat16)

    def share(d, received=False):
        peer = (mine + d) % freqs
        back = (mine - d + freqs) % freqs
        taken = outgoing.at[pl.ds(pl.multiple_of(peer * part, part), part)]
        landing = back if received else mine
        return pltpu.make_async_remote_copy(
            src_ref=taken,
            dst_ref=arrived.at[pl.ds(pl.multiple_of(landing * part, part), part)],
            send_sem=sf.at[d],
            recv_sem=rf.at[d],
            device_id={"freq": peer},
            device_id_type=MESH,
        )

    for d in range(1, freqs):
        share(d).start()
    here = pl.ds(pl.multiple_of(mine * part, part), part)
    keep = pltpu.make_async_copy(outgoing.at[here], arrived.at[here], local.at[0])
    keep.start()
    for link in SENDS:
        for k in range(COUNT[link]):
            copy(link, k).wait_send()
    keep.wait()
    for d in range(1, freqs):
        share(d, True).wait_recv()

    stacked = jnp.concatenate([arrived[:, :half], arrived[:, half:]], 0)
    mixed = jnp.dot(mix[...], stacked, preferred_element_type=jnp.float32)
    for g in range(2 * rows // half):
        span = pl.ds(g * half, half)
        out_ref[span, :] = mixed[g * half : (g + 1) * half, :].T.astype(jnp.bfloat16)
    for d in range(1, freqs):
        share(d).wait_send()


def transform_kernel(spectra_ref, table_ref, out_ref):
    coefs = table_ref.shape[0] // 2
    each = spectra_ref.shape[1] // coefs
    groups, count, width, times = out_ref.shape
    step = pl.program_id(0)
    high, low = table_ref[:coefs, :], table_ref[coefs:, :]
    full = jnp.concatenate([high] * each + [low] * each, 0)
    row = lax.broadcasted_iota(jnp.int32, full.shape, 0)
    left = jnp.concatenate([spectra_ref[...], spectra_ref[...]], 1)
    for u in range(count):
        here = (row // coefs) % each == step * count + u
        right = jnp.where(here, full, 0.0).astype(jnp.bfloat16)
        value = jnp.dot(left, right, preferred_element_type=jnp.float32)
        out_ref[:, u] = value.astype(jnp.bfloat16).reshape(groups, width, times)


def body(freqs, receivers, data, block_of_slot, receiver_order):
    rows, depth = receivers.shape[3], receivers.shape[4]
    points, width = data.shape[2], data.shape[3]
    slots = block_of_slot.shape[0]
    part = rows // freqs
    copies = sum(COUNT.values())
    moved = pl.pallas_call(
        functools.partial(gather_kernel, freqs),
        out_shape=jax.ShapeDtypeStruct((2 * rows, width), jnp.bfloat16),
        in_specs=[
            pl.BlockSpec(memory_space=pltpu.SMEM),
            pl.BlockSpec(memory_space=pltpu.VMEM),
            pl.BlockSpec(memory_space=pl.ANY),
            pl.BlockSpec(memory_space=pl.ANY),
        ],
        out_specs=pl.BlockSpec(memory_space=pltpu.VMEM),
        scratch_shapes=[
            pltpu.VMEM((slots, 2 * rows, depth), jnp.bfloat16),
            pltpu.VMEM((2, slots, depth, width), jnp.bfloat16),
            pltpu.VMEM((2 * rows, 2 * width), jnp.float32),
            pltpu.VMEM((rows, rows), jnp.bfloat16),
            pltpu.VMEM((2 * rows, 2 * rows), jnp.bfloat16),
            pltpu.VMEM((rows, 2 * width), jnp.bfloat16),
            pltpu.VMEM((rows, 2 * width), jnp.bfloat16),
            pltpu.SemaphoreType.DMA((copies,)),
            pltpu.SemaphoreType.DMA((copies,)),
            pltpu.SemaphoreType.DMA((freqs,)),
            pltpu.SemaphoreType.DMA((freqs,)),
            pltpu.SemaphoreType.DMA((2,)),
            pltpu.SemaphoreType.REGULAR((3,)),
        ],
        compiler_params=pltpu.CompilerParams(
            collective_id=0, has_side_effects=True, vmem_limit_bytes=60 * 2**20
        ),
        name="gather_multiply_exchange",
    )(
        block_of_slot,
        receiver_order.reshape(1, rows),
        receivers.reshape(2 * rows, depth),
        data.reshape(2, slots, points // slots, width),
    )
    table = jnp.asarray(tables(freqs))
    each = width // (2 * freqs)
    groups = part // each
    traces = pl.pallas_call(
        transform_kernel,
        out_shape=jax.ShapeDtypeStruct((groups, each, width, NT), jnp.bfloat16),
        grid=(2,),
        in_specs=[
            pl.BlockSpec(moved.shape, lambda i: (0, 0)),
            pl.BlockSpec(table.shape, lambda i: (0, 0)),
        ],
        out_specs=pl.BlockSpec((groups, each // 2, width, NT), lambda i: (0, i, 0, 0)),
        name="transform",
    )(moved, table)
    return traces.reshape(part, width, NT)


def solution(mesh):
    placed = (P("freq", "src", None, None, None), P("freq", None, None, "src"), P(), P())
    return jax.shard_map(
        functools.partial(body, mesh.shape["freq"]),
        mesh=mesh,
        in_specs=placed,
        out_specs=P("freq", "src", None),
        check_vma=False,
    )
```

```python
import functools
import math

import jax
import jax.numpy as jnp
import numpy as np
from jax import lax
from jax.experimental import pallas as pl
from jax.experimental.pallas import tpu as pltpu
from jax.sharding import PartitionSpec as P

NT = 256
MESH = pl.DeviceIdType.MESH
CHUNK = 64
PLACES = [(2, 1), (1, 1), (3, 1), (2, 0), (0, 1), (1, 0), (3, 0), (0, 0)]

LOW, HIGH, EDGE = (0, 256), (256, 256), 80
AROUND = [(0, 1, EDGE, 2 * CHUNK - EDGE)] + [(0, 1, p * CHUNK, CHUNK) for p in range(2, 8)]
SENDS = {
    "xp": [(0, 0, *LOW), (0, 0, *HIGH)] + [(-1, 0, k * CHUNK, CHUNK) for k in range(4)] + AROUND,
    "xm": [(0, 0, *HIGH), (0, 0, *LOW)] + [(1, 0, k * CHUNK, CHUNK) for k in range(4, 8)] + AROUND,
    "z": [(0, 0, *LOW), (0, 0, *HIGH), (-1, 0, 0, EDGE), (1, 0, 0, EDGE)]
    + [(2, 0, p * CHUNK, CHUNK) for p in range(8)],
    "c": [(0, 0, *LOW), (0, 0, *HIGH)]
    + [(-1, 0, *LOW), (1, 0, *HIGH), (0, 1, *LOW)]
    + [(-1, 0, *HIGH), (1, 0, *LOW), (0, 1, *HIGH)]
    + [(2, 0, *LOW), (2, 0, *HIGH)]
    + [(dx, 1, p * CHUNK, CHUNK) for p in range(8) for dx in (-1, 1, 2)],
}
SHIFT = {"xp": (-1, 0, 0), "xm": (1, 0, 0), "z": (0, 1, 0), "c": (0, 0, 1)}
COUNT = {link: len(rows) for link, rows in SENDS.items()}


def tables(count):
    times = np.arange(NT)
    bins = (2 * np.arange(count) + 1) * (NT // (4 * count))
    angle = (bins[:, None] * times[None, :] % NT) * (2.0 * math.pi / NT)
    full = np.stack([np.cos(angle), -np.sin(angle)], 1) * count ** (-0.5)
    full = full.reshape(2 * count, NT).astype(np.float32)
    high = full.astype(jnp.bfloat16).astype(np.float32)
    low = (full - high).astype(jnp.bfloat16).astype(np.float32)
    return np.concatenate([high, low], 0)


def gather_kernel(
    freqs, block_ref, order_ref, own_hbm, data_hbm, out_ref,
    held, data, raw, acc, perm, mix, outgoing, arrived,
    sx, rx, sf, rf, local, known,
):
    me = lax.axis_index("src")
    mine = lax.axis_index("freq")
    x, z, c = me // 4, (me // 2) % 2, me % 2
    depth = own_hbm.shape[1]
    rows = own_hbm.shape[0] // 2
    part = rows // freqs

    def slot(dx, dz, dc):
        return ((x + dx + 4) % 4) * 4 + ((z + dz) % 2) * 2 + (c + dc) % 2

    target = {"xp": slot(1, 0, 0), "xm": slot(-1, 0, 0), "z": slot(0, 1, 0), "c": slot(0, 0, 1)}
    first = {}
    at = 0
    for link in SENDS:
        first[link] = at
        at += COUNT[link]

    def place(p, sign=1):
        dy, dz = PLACES[p]
        return ((mine // 2 + sign * dy + 4) % 4) * 2 + (mine % 2 + dz) % 2

    own_copy = pltpu.make_async_copy(own_hbm, raw, local.at[0])
    data_copy = pltpu.make_async_copy(data_hbm, data, local.at[1])
    own_copy.start()
    data_copy.start()

    barrier = pltpu.get_barrier_semaphore()
    for link in SENDS:
        pl.semaphore_signal(barrier, inc=1, device_id={"src": target[link]}, device_id_type=MESH)
    after, before = {"freq": (mine + 2) % freqs}, {"freq": (mine + freqs - 2) % freqs}
    inner, outer = {"src": target["z"]}, {"src": target["z"], "freq": mine + 1 - 2 * (mine % 2)}
    for peer in (after, before, outer):
        pl.semaphore_signal(barrier, inc=1, device_id=peer, device_id_type=MESH)

    ids = lax.broadcasted_iota(jnp.int32, (rows, rows), 0)
    chosen = jnp.where(ids == order_ref[...], 1.0, 0.0).astype(jnp.float32)
    perm[...] = chosen.T.astype(jnp.bfloat16)
    picks = jnp.concatenate(
        [perm[pl.ds(pl.multiple_of(place(p) * part, part), part), :] for p in range(freqs)], 0
    )
    own_copy.wait()
    for ri in range(2):
        sorted_rows = jnp.dot(picks, raw[ri * rows : (ri + 1) * rows, :], preferred_element_type=jnp.float32)
        for p in range(freqs):
            held[me, pl.ds(p * CHUNK + ri * part, part), :] = sorted_rows[p * part : (p + 1) * part].astype(jnp.bfloat16)
    pl.semaphore_wait(barrier, len(SENDS) + 3)

    rounds = ((before, inner), (before, after), (before,))

    def tell(k):
        for peer in rounds[k]:
            pl.semaphore_signal(known.at[k], inc=1, device_id=peer, device_id_type=MESH)

    def hear(k):
        pl.semaphore_wait(known.at[k], len(rounds[k]))

    def copy(link, k, received=False):
        dx, dz, low, count = SENDS[link][k]
        dc = 0
        if received:
            sx_, sz_, dc = SHIFT[link]
            dx, dz = dx + sx_, dz + sz_
        piece = held.at[slot(dx, dz, dc), pl.ds(low, count)]
        return pltpu.make_async_remote_copy(
            src_ref=piece,
            dst_ref=piece,
            send_sem=sx.at[first[link] + k],
            recv_sem=rx.at[first[link] + k],
            device_id={"src": target[link]},
            device_id_type=MESH,
        )

    def send(link, *which):
        for k in which:
            copy(link, k).start()

    def wait(link, *which):
        for k in which:
            copy(link, k, True).wait_recv()

    def product(dx, dz, dc, low, count, fresh=False):
        j = slot(dx, dz, dc)
        block = block_ref[j]
        right = jnp.concatenate([data[0, block], data[1, block]], 1)
        span = pl.ds(low, count)
        value = jnp.dot(held[j, span, :], right, preferred_element_type=jnp.float32)
        if fresh:
            acc[span, :] = value
        else:
            acc[span, :] += value

    def finish(p):
        mid, half = p * CHUNK + part, acc.shape[1] // 2
        top, low = acc[p * CHUNK : mid, :], acc[mid : mid + part, :]
        real = top[:, :half] - low[:, half:]
        imag = top[:, half:] + low[:, :half]
        return jnp.concatenate([real, imag], 1).astype(jnp.bfloat16)

    def share(p, received=False):
        landing = place(p, -1) if received else mine
        return pltpu.make_async_remote_copy(
            src_ref=outgoing.at[pl.ds(p * part, part)],
            dst_ref=arrived.at[pl.ds(pl.multiple_of(landing * part, part), part)],
            send_sem=sf.at[p],
            recv_sem=rf.at[p],
            device_id={"freq": place(p)},
            device_id_type=MESH,
        )

    send("xp", 0)
    send("xm", 0)
    send("z", 0)
    send("xp", 1)
    send("xm", 1)
    send("z", 1)
    send("c", 0, 1)
    tell(0)

    n = lax.broadcasted_iota(jnp.int32, (2 * rows, 1), 0)
    source = (n % 2) * rows + ((n // 2) % freqs) * part + n // (2 * freqs)
    m = lax.broadcasted_iota(jnp.int32, (2 * rows, 2 * rows), 1)
    mix[...] = jnp.where(m == source, 1.0, 0.0).astype(jnp.bfloat16)

    data_copy.wait()
    product(0, 0, 0, 0, 2 * rows, fresh=True)
    wait("c", 0, 1)
    product(0, 0, 1, 0, 2 * rows)

    wait("xp", 0)
    send("xp", 2, 3, 4, 5)
    send("z", 2)
    send("c", 2)
    wait("xm", 0)
    send("xm", 2, 3, 4, 5)
    send("c", 3)
    wait("z", 0)
    send("c", 4)
    product(-1, 0, 0, *LOW)
    product(1, 0, 0, *HIGH)
    product(0, 1, 0, *LOW)
    hear(0)
    tell(1)
    wait("c", 2, 3, 4)
    product(-1, 0, 1, *LOW)
    product(1, 0, 1, *HIGH)
    product(0, 1, 1, *LOW)

    wait("xm", 1)
    send("z", 3)
    wait("z", 1)
    send("xp", *range(6, 13))
    send("xm", *range(6, 13))
    wait("xp", 1)
    send("c", 5, 6, 7)
    product(-1, 0, 0, *HIGH)
    product(1, 0, 0, *LOW)
    product(0, 1, 0, *HIGH)
    hear(1)
    tell(2)
    wait("c", 5, 6, 7)
    hear(2)

    for k in range(4):
        wait("xp", 2 + k)
        send("z", 4 + k)
        if k == 0:
            product(-1, 0, 1, *HIGH)
            product(1, 0, 1, *LOW)
            product(0, 1, 1, *HIGH)
    send("c", 8)
    for k in range(4):
        wait("xm", 2 + k)
        send("z", 8 + k)
    send("c", 9)
    product(2, 0, 0, 0, 2 * rows)
    wait("c", 8, 9)
    product(2, 0, 1, 0, 2 * rows)

    here = pl.ds(pl.multiple_of(mine * part, part), part)
    for p in range(freqs + 1):
        if p < freqs:
            if p == 0:
                wait("z", 2, 3)
            else:
                wait("xp", 5 + p)
                send("c", 10 + 3 * p)
                wait("xm", 5 + p)
                send("c", 11 + 3 * p)
            if p == 0:
                send("c", 10, 11)
            wait("z", 4 + p)
            send("c", 12 + 3 * p)
            for dx in (-1, 1, 2):
                product(dx, 1, 0, p * CHUNK, CHUNK)
        if p > 0:
            last = p - 1
            for k, dx in enumerate((-1, 1, 2)):
                wait("c", 10 + 3 * last + k)
                product(dx, 1, 1, last * CHUNK, CHUNK)
            if last < freqs - 1:
                outgoing[pl.ds(last * part, part), :] = finish(last)
                share(last).start()
            else:
                arrived[here, :] = finish(last)
    for link in SENDS:
        for k in range(COUNT[link]):
            copy(link, k).wait_send()
    for p in range(freqs - 1):
        share(p, True).wait_recv()

    half = acc.shape[1] // 2
    stacked = jnp.concatenate([arrived[:, :half], arrived[:, half:]], 0)
    mixed = jnp.dot(mix[...], stacked, preferred_element_type=jnp.float32)
    for g in range(2 * rows // half):
        span = pl.ds(g * half, half)
        out_ref[span, :] = mixed[g * half : (g + 1) * half, :].T.astype(jnp.bfloat16)
    for p in range(freqs - 1):
        share(p).wait_send()


def transform_kernel(spectra_ref, table_ref, out_ref):
    coefs = table_ref.shape[0] // 2
    each = spectra_ref.shape[1] // coefs
    groups, count, width, times = out_ref.shape
    step = pl.program_id(0)
    high, low = table_ref[:coefs, :], table_ref[coefs:, :]
    full = jnp.concatenate([high] * each + [low] * each, 0)
    row = lax.broadcasted_iota(jnp.int32, full.shape, 0)
    left = jnp.concatenate([spectra_ref[...], spectra_ref[...]], 1)
    for u in range(count):
        here = (row // coefs) % each == step * count + u
        right = jnp.where(here, full, 0.0).astype(jnp.bfloat16)
        value = jnp.dot(left, right, preferred_element_type=jnp.float32)
        out_ref[:, u] = value.astype(jnp.bfloat16).reshape(groups, width, times)


def body(freqs, receivers, data, block_of_slot, receiver_order):
    rows, depth = receivers.shape[3], receivers.shape[4]
    points, width = data.shape[2], data.shape[3]
    slots = block_of_slot.shape[0]
    part = rows // freqs
    copies = sum(COUNT.values())
    moved = pl.pallas_call(
        functools.partial(gather_kernel, freqs),
        out_shape=jax.ShapeDtypeStruct((2 * rows, width), jnp.bfloat16),
        in_specs=[
            pl.BlockSpec(memory_space=pltpu.SMEM),
            pl.BlockSpec(memory_space=pltpu.VMEM),
            pl.BlockSpec(memory_space=pl.ANY),
            pl.BlockSpec(memory_space=pl.ANY),
        ],
        out_specs=pl.BlockSpec(memory_space=pltpu.VMEM),
        scratch_shapes=[
            pltpu.VMEM((slots, 2 * rows, depth), jnp.bfloat16),
            pltpu.VMEM((2, slots, depth, width), jnp.bfloat16),
            pltpu.VMEM((2 * rows, depth), jnp.bfloat16),
            pltpu.VMEM((2 * rows, 2 * width), jnp.float32),
            pltpu.VMEM((rows, rows), jnp.bfloat16),
            pltpu.VMEM((2 * rows, 2 * rows), jnp.bfloat16),
            pltpu.VMEM((rows, 2 * width), jnp.bfloat16),
            pltpu.VMEM((rows, 2 * width), jnp.bfloat16),
            pltpu.SemaphoreType.DMA((copies,)),
            pltpu.SemaphoreType.DMA((copies,)),
            pltpu.SemaphoreType.DMA((freqs,)),
            pltpu.SemaphoreType.DMA((freqs,)),
            pltpu.SemaphoreType.DMA((2,)),
            pltpu.SemaphoreType.REGULAR((3,)),
        ],
        compiler_params=pltpu.CompilerParams(
            collective_id=0, has_side_effects=True, vmem_limit_bytes=60 * 2**20
        ),
        name="gather_multiply_exchange",
    )(
        block_of_slot,
        receiver_order.reshape(1, rows),
        receivers.reshape(2 * rows, depth),
        data.reshape(2, slots, points // slots, width),
    )
    table = jnp.asarray(tables(freqs))
    each = width // (2 * freqs)
    groups = part // each
    traces = pl.pallas_call(
        transform_kernel,
        out_shape=jax.ShapeDtypeStruct((groups, each, width, NT), jnp.bfloat16),
        grid=(2,),
        in_specs=[
            pl.BlockSpec(moved.shape, lambda i: (0, 0)),
            pl.BlockSpec(table.shape, lambda i: (0, 0)),
        ],
        out_specs=pl.BlockSpec((groups, each // 2, width, NT), lambda i: (0, i, 0, 0)),
        name="transform",
    )(moved, table)
    return traces.reshape(part, width, NT)


def solution(mesh):
    placed = (P("freq", "src", None, None, None), P("freq", None, None, "src"), P(), P())
    return jax.shard_map(
        functools.partial(body, mesh.shape["freq"]),
        mesh=mesh,
        in_specs=placed,
        out_specs=P("freq", "src", None),
        check_vma=False,
    )
```

```python
import functools
import math

import jax
import jax.numpy as jnp
import numpy as np
from jax import lax
from jax.experimental import pallas as pl
from jax.experimental.pallas import tpu as pltpu
from jax.sharding import PartitionSpec as P

NT = 256
MESH = pl.DeviceIdType.MESH
CHUNK = 64
PLACES = [(2, 1), (1, 1), (3, 1), (2, 0), (0, 1), (1, 0), (3, 0), (0, 0)]

LOW, HIGH, EDGE = (0, 256), (256, 256), 80
AROUND = [(0, 1, EDGE, 2 * CHUNK - EDGE)] + [(0, 1, p * CHUNK, CHUNK) for p in range(2, 8)]
SENDS = {
    "xp": [(0, 0, *LOW), (0, 0, *HIGH)] + [(-1, 0, k * CHUNK, CHUNK) for k in range(4)] + AROUND,
    "xm": [(0, 0, *HIGH), (0, 0, *LOW)] + [(1, 0, k * CHUNK, CHUNK) for k in range(4, 8)] + AROUND,
    "z": [(0, 0, *LOW), (0, 0, *HIGH), (-1, 0, 0, EDGE), (1, 0, 0, EDGE)]
    + [(2, 0, p * CHUNK, CHUNK) for p in range(8)],
    "c": [(0, 0, *LOW), (0, 0, *HIGH)]
    + [(-1, 0, *LOW), (1, 0, *HIGH), (0, 1, *LOW)]
    + [(-1, 0, *HIGH), (1, 0, *LOW), (0, 1, *HIGH)]
    + [(2, 0, *LOW), (2, 0, *HIGH)]
    + [(dx, 1, p * CHUNK, CHUNK) for p in range(8) for dx in (-1, 1, 2)],
}
SHIFT = {"xp": (-1, 0, 0), "xm": (1, 0, 0), "z": (0, 1, 0), "c": (0, 0, 1)}
COUNT = {link: len(rows) for link, rows in SENDS.items()}


def tables(count):
    times = np.arange(NT)
    bins = (2 * np.arange(count) + 1) * (NT // (4 * count))
    angle = (bins[:, None] * times[None, :] % NT) * (2.0 * math.pi / NT)
    full = np.stack([np.cos(angle), -np.sin(angle)], 1) * count ** (-0.5)
    full = full.reshape(2 * count, NT).astype(np.float32)
    high = full.astype(jnp.bfloat16).astype(np.float32)
    low = (full - high).astype(jnp.bfloat16).astype(np.float32)
    return np.concatenate([high, low], 0)


def gather_kernel(
    freqs, block_hbm, order_hbm, own_hbm, data_hbm, out_ref,
    block_ref, order_ref, held, data, raw, acc, perm, mix, outgoing, arrived,
    sx, rx, sf, rf, local, known,
):
    me = lax.axis_index("src")
    mine = lax.axis_index("freq")
    x, z, c = me // 4, (me // 2) % 2, me % 2
    depth = own_hbm.shape[1]
    rows = own_hbm.shape[0] // 2
    part = rows // freqs

    def slot(dx, dz, dc):
        return ((x + dx + 4) % 4) * 4 + ((z + dz) % 2) * 2 + (c + dc) % 2

    target = {"xp": slot(1, 0, 0), "xm": slot(-1, 0, 0), "z": slot(0, 1, 0), "c": slot(0, 0, 1)}
    first = {}
    at = 0
    for link in SENDS:
        first[link] = at
        at += COUNT[link]

    def place(p, sign=1):
        dy, dz = PLACES[p]
        return ((mine // 2 + sign * dy + 4) % 4) * 2 + (mine % 2 + dz) % 2

    barrier = pltpu.get_barrier_semaphore()
    for link in SENDS:
        pl.semaphore_signal(barrier, inc=1, device_id={"src": target[link]}, device_id_type=MESH)
    after, before = {"freq": (mine + 2) % freqs}, {"freq": (mine + freqs - 2) % freqs}
    inner, outer = {"src": target["z"]}, {"src": target["z"], "freq": mine + 1 - 2 * (mine % 2)}
    for peer in (after, before, outer):
        pl.semaphore_signal(barrier, inc=1, device_id=peer, device_id_type=MESH)

    order_copy = pltpu.make_async_copy(order_hbm, order_ref, local.at[2])
    own_copy = pltpu.make_async_copy(own_hbm, raw, local.at[0])
    block_copy = pltpu.make_async_copy(block_hbm, block_ref, local.at[3])
    data_copy = pltpu.make_async_copy(data_hbm, data, local.at[1])
    for one in (order_copy, own_copy, block_copy, data_copy):
        one.start()

    ids = lax.broadcasted_iota(jnp.int32, (rows, rows), 0)
    order_copy.wait()
    chosen = jnp.where(ids == order_ref[...], 1.0, 0.0).astype(jnp.float32)
    perm[...] = chosen.T.astype(jnp.bfloat16)
    picks = jnp.concatenate(
        [perm[pl.ds(pl.multiple_of(place(p) * part, part), part), :] for p in range(freqs)], 0
    )
    own_copy.wait()
    for ri in range(2):
        sorted_rows = jnp.dot(picks, raw[ri * rows : (ri + 1) * rows, :], preferred_element_type=jnp.float32)
        for p in range(freqs):
            held[me, pl.ds(p * CHUNK + ri * part, part), :] = sorted_rows[p * part : (p + 1) * part].astype(jnp.bfloat16)
    pl.semaphore_wait(barrier, len(SENDS) + 3)

    rounds = ((before, inner), (before, after), (before,))

    def tell(k):
        for peer in rounds[k]:
            pl.semaphore_signal(known.at[k], inc=1, device_id=peer, device_id_type=MESH)

    def hear(k):
        pl.semaphore_wait(known.at[k], len(rounds[k]))

    def copy(link, k, received=False):
        dx, dz, low, count = SENDS[link][k]
        dc = 0
        if received:
            sx_, sz_, dc = SHIFT[link]
            dx, dz = dx + sx_, dz + sz_
        piece = held.at[slot(dx, dz, dc), pl.ds(low, count)]
        return pltpu.make_async_remote_copy(
            src_ref=piece,
            dst_ref=piece,
            send_sem=sx.at[first[link] + k],
            recv_sem=rx.at[first[link] + k],
            device_id={"src": target[link]},
            device_id_type=MESH,
        )

    def send(link, *which):
        for k in which:
            copy(link, k).start()

    def wait(link, *which):
        for k in which:
            copy(link, k, True).wait_recv()

    def product(dx, dz, dc, low, count, fresh=False):
        j = slot(dx, dz, dc)
        block = block_ref[j]
        right = jnp.concatenate([data[0, block], data[1, block]], 1)
        span = pl.ds(low, count)
        value = jnp.dot(held[j, span, :], right, preferred_element_type=jnp.float32)
        if fresh:
            acc[span, :] = value
        else:
            acc[span, :] += value

    def finish(p):
        mid, half = p * CHUNK + part, acc.shape[1] // 2
        top, low = acc[p * CHUNK : mid, :], acc[mid : mid + part, :]
        real = top[:, :half] - low[:, half:]
        imag = top[:, half:] + low[:, :half]
        return jnp.concatenate([real, imag], 1).astype(jnp.bfloat16)

    def share(p, received=False):
        landing = place(p, -1) if received else mine
        return pltpu.make_async_remote_copy(
            src_ref=outgoing.at[pl.ds(p * part, part)],
            dst_ref=arrived.at[pl.ds(pl.multiple_of(landing * part, part), part)],
            send_sem=sf.at[p],
            recv_sem=rf.at[p],
            device_id={"freq": place(p)},
            device_id_type=MESH,
        )

    send("xp", 0)
    send("xm", 0)
    send("z", 0)
    send("xp", 1)
    send("xm", 1)
    send("z", 1)
    send("c", 0, 1)
    tell(0)

    n = lax.broadcasted_iota(jnp.int32, (2 * rows, 1), 0)
    source = (n % 2) * rows + ((n // 2) % freqs) * part + n // (2 * freqs)
    m = lax.broadcasted_iota(jnp.int32, (2 * rows, 2 * rows), 1)
    mix[...] = jnp.where(m == source, 1.0, 0.0).astype(jnp.bfloat16)

    block_copy.wait()
    data_copy.wait()
    product(0, 0, 0, 0, 2 * rows, fresh=True)
    wait("c", 0, 1)
    product(0, 0, 1, 0, 2 * rows)

    wait("xp", 0)
    send("xp", 2, 3, 4, 5)
    send("z", 2)
    send("c", 2)
    wait("xm", 0)
    send("xm", 2, 3, 4, 5)
    send("c", 3)
    wait("z", 0)
    send("c", 4)
    product(-1, 0, 0, *LOW)
    product(1, 0, 0, *HIGH)
    product(0, 1, 0, *LOW)
    hear(0)
    tell(1)
    wait("c", 2, 3, 4)
    product(-1, 0, 1, *LOW)
    product(1, 0, 1, *HIGH)
    product(0, 1, 1, *LOW)

    wait("xm", 1)
    send("z", 3)
    wait("z", 1)
    send("xp", *range(6, 13))
    send("xm", *range(6, 13))
    wait("xp", 1)
    send("c", 5, 6, 7)
    product(-1, 0, 0, *HIGH)
    product(1, 0, 0, *LOW)
    product(0, 1, 0, *HIGH)
    hear(1)
    tell(2)
    wait("c", 5, 6, 7)
    hear(2)

    for k in range(4):
        wait("xp", 2 + k)
        send("z", 4 + k)
        if k == 0:
            product(-1, 0, 1, *HIGH)
            product(1, 0, 1, *LOW)
            product(0, 1, 1, *HIGH)
    send("c", 8)
    for k in range(4):
        wait("xm", 2 + k)
        send("z", 8 + k)
    send("c", 9)
    product(2, 0, 0, 0, 2 * rows)
    wait("c", 8, 9)
    product(2, 0, 1, 0, 2 * rows)

    here = pl.ds(pl.multiple_of(mine * part, part), part)
    for p in range(freqs + 1):
        if p < freqs:
            if p == 0:
                wait("z", 2, 3)
            else:
                wait("xp", 5 + p)
                send("c", 10 + 3 * p)
                wait("xm", 5 + p)
                send("c", 11 + 3 * p)
            if p == 0:
                send("c", 10, 11)
            wait("z", 4 + p)
            send("c", 12 + 3 * p)
            for dx in (-1, 1, 2):
                product(dx, 1, 0, p * CHUNK, CHUNK)
        if p > 0:
            last = p - 1
            for k, dx in enumerate((-1, 1, 2)):
                wait("c", 10 + 3 * last + k)
                product(dx, 1, 1, last * CHUNK, CHUNK)
            if last < freqs - 1:
                outgoing[pl.ds(last * part, part), :] = finish(last)
                share(last).start()
            else:
                arrived[here, :] = finish(last)
    for link in SENDS:
        for k in range(COUNT[link]):
            copy(link, k).wait_send()
    for p in range(freqs - 1):
        share(p, True).wait_recv()

    half = acc.shape[1] // 2
    stacked = jnp.concatenate([arrived[:, :half], arrived[:, half:]], 0)
    mixed = jnp.dot(mix[...], stacked, preferred_element_type=jnp.float32)
    for g in range(2 * rows // half):
        span = pl.ds(g * half, half)
        out_ref[span, :] = mixed[g * half : (g + 1) * half, :].T.astype(jnp.bfloat16)
    for p in range(freqs - 1):
        share(p).wait_send()


def transform_kernel(spectra_ref, table_ref, out_hbm, done, sems):
    coefs = table_ref.shape[0] // 2
    each, groups, width, times = done.shape
    high, low = table_ref[:coefs, :], table_ref[coefs:, :]
    full = jnp.concatenate([high] * each + [low] * each, 0)
    row = lax.broadcasted_iota(jnp.int32, full.shape, 0)
    left = jnp.concatenate([spectra_ref[...], spectra_ref[...]], 1)
    copies = []
    for u in range(each):
        here = (row // coefs) % each == u
        right = jnp.where(here, full, 0.0).astype(jnp.bfloat16)
        value = jnp.dot(left, right, preferred_element_type=jnp.float32)
        done[u] = value.astype(jnp.bfloat16).reshape(groups, width, times)
        copies.append(pltpu.make_async_copy(done.at[u], out_hbm.at[:, u], sems.at[u]))
        copies[-1].start()
    for one in copies:
        one.wait()


def body(freqs, receivers, data, block_of_slot, receiver_order):
    rows, depth = receivers.shape[3], receivers.shape[4]
    points, width = data.shape[2], data.shape[3]
    slots = block_of_slot.shape[0]
    part = rows // freqs
    copies = sum(COUNT.values())
    moved = pl.pallas_call(
        functools.partial(gather_kernel, freqs),
        out_shape=jax.ShapeDtypeStruct((2 * rows, width), jnp.bfloat16),
        in_specs=[
            pl.BlockSpec(memory_space=pl.ANY),
            pl.BlockSpec(memory_space=pl.ANY),
            pl.BlockSpec(memory_space=pl.ANY),
            pl.BlockSpec(memory_space=pl.ANY),
        ],
        out_specs=pl.BlockSpec(memory_space=pltpu.VMEM),
        scratch_shapes=[
            pltpu.SMEM((slots,), jnp.int32),
            pltpu.VMEM((1, rows), jnp.int32),
            pltpu.VMEM((slots, 2 * rows, depth), jnp.bfloat16),
            pltpu.VMEM((2, slots, depth, width), jnp.bfloat16),
            pltpu.VMEM((2 * rows, depth), jnp.bfloat16),
            pltpu.VMEM((2 * rows, 2 * width), jnp.float32),
            pltpu.VMEM((rows, rows), jnp.bfloat16),
            pltpu.VMEM((2 * rows, 2 * rows), jnp.bfloat16),
            pltpu.VMEM((rows, 2 * width), jnp.bfloat16),
            pltpu.VMEM((rows, 2 * width), jnp.bfloat16),
            pltpu.SemaphoreType.DMA((copies,)),
            pltpu.SemaphoreType.DMA((copies,)),
            pltpu.SemaphoreType.DMA((freqs,)),
            pltpu.SemaphoreType.DMA((freqs,)),
            pltpu.SemaphoreType.DMA((4,)),
            pltpu.SemaphoreType.REGULAR((3,)),
        ],
        compiler_params=pltpu.CompilerParams(
            collective_id=0, has_side_effects=True, vmem_limit_bytes=60 * 2**20
        ),
        name="gather_multiply_exchange",
    )(
        block_of_slot,
        receiver_order.reshape(1, rows),
        receivers.reshape(2 * rows, depth),
        data.reshape(2, slots, points // slots, width),
    )
    table = jnp.asarray(tables(freqs))
    each = width // (2 * freqs)
    groups = part // each
    traces = pl.pallas_call(
        transform_kernel,
        out_shape=jax.ShapeDtypeStruct((groups, each, width, NT), jnp.bfloat16),
        in_specs=[pl.BlockSpec(memory_space=pltpu.VMEM)] * 2,
        out_specs=pl.BlockSpec(memory_space=pl.ANY),
        scratch_shapes=[
            pltpu.VMEM((each, groups, width, NT), jnp.bfloat16),
            pltpu.SemaphoreType.DMA((each,)),
        ],
        name="transform",
    )(moved, table)
    return traces.reshape(part, width, NT)


def solution(mesh):
    placed = (P("freq", "src", None, None, None), P("freq", None, None, "src"), P(), P())
    return jax.shard_map(
        functools.partial(body, mesh.shape["freq"]),
        mesh=mesh,
        in_specs=placed,
        out_specs=P("freq", "src", None),
        check_vma=False,
    )
```

```python
import functools
import math

import jax
import jax.numpy as jnp
import numpy as np
from jax import lax
from jax.experimental import pallas as pl
from jax.experimental.pallas import tpu as pltpu
from jax.sharding import PartitionSpec as P

NT = 256
MESH = pl.DeviceIdType.MESH
CHUNK = 64


def sending_order(y_size, halves):
    def late(f):
        return 0.8 * (f // halves) + 2.2 * (f % halves)

    def need(f, q):
        dy = abs(f // halves - q // halves)
        hops = min(dy, y_size - dy) + 2 * (f % halves != q % halves)
        return 0.75 * hops + late(f) - late(q)

    count = y_size * halves
    return [sorted((q for q in range(count) if q != f), key=lambda q: -need(f, q)) + [f] for f in range(count)]


ORDER = sending_order(4, 2)

LOW, HIGH, EDGE = (0, 256), (256, 256), 80
AROUND = [(0, 1, EDGE, 2 * CHUNK - EDGE)] + [(0, 1, p * CHUNK, CHUNK) for p in range(2, 8)]
SENDS = {
    "xp": [(0, 0, *LOW), (0, 0, 256, 128)]
    + [(-1, 0, k * CHUNK, CHUNK) for k in range(4)]
    + [(0, 0, 384, 128)]
    + AROUND,
    "xm": [(0, 0, *LOW), (0, 0, *HIGH)]
    + AROUND[:2]
    + [(1, 0, k * CHUNK, CHUNK) for k in range(4, 8)]
    + AROUND[2:],
    "z": [(0, 0, *LOW), (0, 0, *HIGH), (-1, 0, 0, EDGE), (1, 0, 0, EDGE)]
    + [(2, 0, p * CHUNK, CHUNK) for p in range(8)],
    "c": [(0, 0, *LOW), (0, 0, *HIGH)]
    + [(-1, 0, *LOW), (1, 0, *LOW), (0, 1, *LOW)]
    + [(1, 0, *HIGH), (0, 1, *HIGH), (-1, 0, *HIGH)]
    + [(2, 0, *LOW), (2, 0, *HIGH)]
    + [(dx, 1, p * CHUNK, CHUNK) for p in range(8) for dx in (-1, 1, 2)],
}
SHIFT = {"xp": (-1, 0, 0), "xm": (1, 0, 0), "z": (0, 1, 0), "c": (0, 0, 1)}
COUNT = {link: len(rows) for link, rows in SENDS.items()}


def tables(count):
    times = np.arange(NT)
    bins = (2 * np.arange(count) + 1) * (NT // (4 * count))
    angle = (bins[:, None] * times[None, :] % NT) * (2.0 * math.pi / NT)
    full = np.stack([np.cos(angle), -np.sin(angle)], 1) * count ** (-0.5)
    full = full.reshape(2 * count, NT).astype(np.float32)
    high = full.astype(jnp.bfloat16).astype(np.float32)
    low = (full - high).astype(jnp.bfloat16).astype(np.float32)
    return np.concatenate([high, low], 0)


def gather_kernel(
    freqs, block_hbm, order_hbm, own_hbm, data_hbm, out_ref,
    block_ref, order_ref, held, data, raw, acc, perm, mix, outgoing, arrived,
    sx, rx, sf, rf, local, known,
):
    me = lax.axis_index("src")
    mine = lax.axis_index("freq")
    x, z, c = me // 4, (me // 2) % 2, me % 2
    depth = own_hbm.shape[1]
    rows = own_hbm.shape[0] // 2
    part = rows // freqs

    def slot(dx, dz, dc):
        return ((x + dx + 4) % 4) * 4 + ((z + dz) % 2) * 2 + (c + dc) % 2

    target = {"xp": slot(1, 0, 0), "xm": slot(-1, 0, 0), "z": slot(0, 1, 0), "c": slot(0, 0, 1)}
    first = {}
    at = 0
    for link in SENDS:
        first[link] = at
        at += COUNT[link]

    def place(p):
        if p == freqs - 1:
            return mine
        return sum(jnp.where(mine == f, ORDER[f][p], 0) for f in range(freqs))

    farther = {"xp": x < 3, "xm": x == 0, "z": z == 0, "c": c == 1}
    y, upper = mine // 2, mine % 2
    below = [(y == 0, 2 + upper), (y == 0, 6 + upper), (y == 1, 4 + upper), (mine == 0, 1)]
    above = jnp.where(y == 0, 0, jnp.where(y == 2, 2, 0) + upper)

    def one(flag):
        return jnp.where(flag, 1, 0)

    def greet(semaphore, peer):
        pl.semaphore_signal(semaphore, inc=1, device_id=peer, device_id_type=MESH)

    barrier = pltpu.get_barrier_semaphore()
    for link in SENDS:
        pl.when(farther[link])(functools.partial(greet, barrier, {"src": target[link]}))
    for flag, peer in below:
        pl.when(flag)(functools.partial(greet, barrier, {"freq": peer}))
    order_copy = pltpu.make_async_copy(order_hbm, order_ref, local.at[2])
    own_copy = pltpu.make_async_copy(own_hbm, raw, local.at[0])
    block_copy = pltpu.make_async_copy(block_hbm, block_ref, local.at[3])
    data_copy = pltpu.make_async_copy(data_hbm, data, local.at[1])
    for begun in (order_copy, own_copy, block_copy, data_copy):
        begun.start()
    nearer = sum(1 - one(farther[link]) for link in SENDS) + one(mine > 0)

    def enter():
        pl.semaphore_wait(barrier, nearer)

    pl.when(nearer > 0)(enter)
    for k, (link, far) in enumerate((("xp", "xm"), ("xm", "xp"), ("z", "z"), ("c", "c"))):
        pl.when(jnp.logical_not(farther[far]))(functools.partial(greet, known.at[k], {"src": target[far]}))

    peers_below = sum(one(flag) for flag, _ in below)

    def report():
        pl.when(peers_below > 0)(lambda: pl.semaphore_wait(known.at[4], peers_below))
        pl.when(mine > 0)(functools.partial(greet, known.at[4], {"freq": above}))

    def spread():
        pl.when(mine > 0)(lambda: pl.semaphore_wait(known.at[5], 1))
        for flag, peer in below:
            pl.when(flag)(functools.partial(greet, known.at[5], {"freq": peer}))

    def copy(link, k, received=False):
        dx, dz, low, count = SENDS[link][k]
        dc = 0
        if received:
            sx_, sz_, dc = SHIFT[link]
            dx, dz = dx + sx_, dz + sz_
        piece = held.at[slot(dx, dz, dc), pl.ds(low, count)]
        return pltpu.make_async_remote_copy(
            src_ref=piece,
            dst_ref=piece,
            send_sem=sx.at[first[link] + k],
            recv_sem=rx.at[first[link] + k],
            device_id={"src": target[link]},
            device_id_type=MESH,
        )

    def send(link, *which):
        for k in which:
            copy(link, k).start()

    def wait(link, *which):
        for k in which:
            copy(link, k, True).wait_recv()

    def product(blocks, low, count, fresh=False):
        span = pl.ds(low, count)
        value = 0.0 if fresh else acc[span, :]
        for dx, dz, dc in blocks:
            j = slot(dx, dz, dc)
            block = block_ref[j]
            right = jnp.concatenate([data[0, block], data[1, block]], 1)
            value += jnp.dot(held[j, span, :], right, preferred_element_type=jnp.float32)
        acc[span, :] = value

    def finish(p):
        mid, half = p * CHUNK + part, acc.shape[1] // 2
        top, low = acc[p * CHUNK : mid, :], acc[mid : mid + part, :]
        real = top[:, :half] - low[:, half:]
        imag = top[:, half:] + low[:, :half]
        return jnp.concatenate([real, imag], 1).astype(jnp.bfloat16)

    def share(p, sender=mine):
        return pltpu.make_async_remote_copy(
            src_ref=outgoing.at[pl.ds(p * part, part)],
            dst_ref=arrived.at[pl.ds(pl.multiple_of(sender * part, part), part)],
            send_sem=sf.at[p],
            recv_sem=rf.at[sender],
            device_id={"freq": place(p)},
            device_id_type=MESH,
        )

    order_copy.wait()
    ids = lax.broadcasted_iota(jnp.int32, (rows, rows), 0)
    chosen = jnp.where(ids == order_ref[...], 1.0, 0.0).astype(jnp.float32)
    perm[...] = chosen.T.astype(jnp.bfloat16)
    own_copy.wait()
    for side in range(2):
        group = range(side * freqs // 2, (side + 1) * freqs // 2)
        picks = jnp.concatenate(
            [perm[pl.ds(pl.multiple_of(place(p) * part, part), part), :] for p in group], 0
        )
        for ri in range(2):
            wide = jnp.dot(picks, raw[ri * rows : (ri + 1) * rows, :], preferred_element_type=jnp.float32)
            for k, p in enumerate(group):
                held[me, pl.ds(p * CHUNK + ri * part, part), :] = wide[k * part : (k + 1) * part].astype(jnp.bfloat16)
    for near in (True, False):
        for k, link in enumerate(("xp", "xm", "z")):

            def begin(k=k, link=link, near=near):
                if not near:
                    pl.semaphore_wait(known.at[k], 1)
                send(link, 0, 1)

            pl.when(jnp.logical_not(farther[link]) if near else farther[link])(begin)
    pl.when(farther["c"])(lambda: pl.semaphore_wait(known.at[3], 1))
    send("c", 0, 1)

    n = lax.broadcasted_iota(jnp.int32, (2 * rows, 1), 0)
    source = (n % 2) * rows + ((n // 2) % freqs) * part + n // (2 * freqs)
    m = lax.broadcasted_iota(jnp.int32, (2 * rows, 2 * rows), 1)
    mix[...] = jnp.where(m == source, 1.0, 0.0).astype(jnp.bfloat16)

    block_copy.wait()
    data_copy.wait()
    product([(0, 0, 0)], 0, 2 * rows, fresh=True)

    wait("xp", 0)
    send("xp", 2, 3, 4, 5, 6)
    send("z", 2)
    wait("xm", 0)
    send("z", 3)
    wait("z", 0)
    send("xm", 2, 3)
    send("c", 2, 3, 4)
    wait("c", 0, 1)
    product([(0, 0, 1)], 0, 2 * rows)
    product([(-1, 0, 0), (1, 0, 0), (0, 1, 0)], *LOW)
    report()
    wait("c", 2, 3, 4)
    product([(-1, 0, 1), (1, 0, 1), (0, 1, 1)], *LOW)

    for k in range(2):
        wait("xp", 2 + k)
        send("z", 4 + k)
    wait("xm", 1)
    send("xm", 4, 5, 6, 7)
    wait("z", 1)
    send("xm", *range(8, 13))
    send("xp", *range(7, 14))
    send("c", 5, 6)
    product([(1, 0, 0), (0, 1, 0)], *HIGH)
    for k in range(2, 4):
        wait("xp", 2 + k)
        send("z", 4 + k)
    send("c", 8)
    wait("c", 5, 6)
    product([(1, 0, 1), (0, 1, 1)], *HIGH)
    product([(2, 0, 0)], *LOW)
    wait("xp", 1, 6)
    send("c", 7)
    product([(-1, 0, 0)], *HIGH)
    spread()
    for k in range(4):
        wait("xm", 4 + k)
        send("z", 8 + k)
    send("c", 9)
    product([(2, 0, 0)], *HIGH)
    wait("c", 7, 8, 9)
    product([(2, 0, 1)], *LOW)
    product([(-1, 0, 1), (2, 0, 1)], *HIGH)

    sides = (-1, 1, 2)
    here = pl.ds(pl.multiple_of(mine * part, part), part)
    for p in range(freqs + 1):
        if p < freqs:
            if p == 0:
                wait("z", 2, 3)
                send("c", 10, 11)
            else:
                wait("xp", 6 + p)
                send("c", 10 + 3 * p)
                wait("xm", 1 + p if p < 3 else 5 + p)
                send("c", 11 + 3 * p)
            wait("z", 4 + p)
            send("c", 12 + 3 * p)
            product([(dx, 1, 0) for dx in sides], p * CHUNK, CHUNK)
        if p > 0:
            last = p - 1
            wait("c", *range(10 + 3 * last, 13 + 3 * last))
            product([(dx, 1, 1) for dx in sides], last * CHUNK, CHUNK)
            if last < freqs - 1:
                outgoing[pl.ds(last * part, part), :] = finish(last)
                share(last).start()
            else:
                arrived[here, :] = finish(last)
    for link in SENDS:
        for k in range(COUNT[link]):
            copy(link, k).wait_send()
    for p in range(freqs - 1):
        share(p, (mine + 1 + p) % freqs).wait_recv()

    half = acc.shape[1] // 2
    stacked = jnp.concatenate([arrived[:, :half], arrived[:, half:]], 0)
    mixed = jnp.dot(mix[...], stacked, preferred_element_type=jnp.float32)
    for g in range(2 * rows // half):
        span = pl.ds(g * half, half)
        out_ref[span, :] = mixed[g * half : (g + 1) * half, :].T.astype(jnp.bfloat16)
    for p in range(freqs - 1):
        share(p).wait_send()


def transform_kernel(spectra_ref, table_ref, out_hbm, done, sems):
    coefs = table_ref.shape[0] // 2
    each, groups, width, times = done.shape
    high, low = table_ref[:coefs, :], table_ref[coefs:, :]
    full = jnp.concatenate([high] * each + [low] * each, 0)
    row = lax.broadcasted_iota(jnp.int32, full.shape, 0)
    left = jnp.concatenate([spectra_ref[...], spectra_ref[...]], 1)
    copies = []
    for u in range(each):
        here = (row // coefs) % each == u
        right = jnp.where(here, full, 0.0).astype(jnp.bfloat16)
        value = jnp.dot(left, right, preferred_element_type=jnp.float32)
        done[u] = value.astype(jnp.bfloat16).reshape(groups, width, times)
        copies.append(pltpu.make_async_copy(done.at[u], out_hbm.at[:, u], sems.at[u]))
        copies[-1].start()
    for one in copies:
        one.wait()


def body(freqs, receivers, data, block_of_slot, receiver_order):
    rows, depth = receivers.shape[3], receivers.shape[4]
    points, width = data.shape[2], data.shape[3]
    slots = block_of_slot.shape[0]
    part = rows // freqs
    copies = sum(COUNT.values())
    moved = pl.pallas_call(
        functools.partial(gather_kernel, freqs),
        out_shape=jax.ShapeDtypeStruct((2 * rows, width), jnp.bfloat16),
        in_specs=[
            pl.BlockSpec(memory_space=pl.ANY),
            pl.BlockSpec(memory_space=pl.ANY),
            pl.BlockSpec(memory_space=pl.ANY),
            pl.BlockSpec(memory_space=pl.ANY),
        ],
        out_specs=pl.BlockSpec(memory_space=pltpu.VMEM),
        scratch_shapes=[
            pltpu.SMEM((slots,), jnp.int32),
            pltpu.VMEM((1, rows), jnp.int32),
            pltpu.VMEM((slots, 2 * rows, depth), jnp.bfloat16),
            pltpu.VMEM((2, slots, depth, width), jnp.bfloat16),
            pltpu.VMEM((2 * rows, depth), jnp.bfloat16),
            pltpu.VMEM((2 * rows, 2 * width), jnp.float32),
            pltpu.VMEM((rows, rows), jnp.bfloat16),
            pltpu.VMEM((2 * rows, 2 * rows), jnp.bfloat16),
            pltpu.VMEM((rows, 2 * width), jnp.bfloat16),
            pltpu.VMEM((rows, 2 * width), jnp.bfloat16),
            pltpu.SemaphoreType.DMA((copies,)),
            pltpu.SemaphoreType.DMA((copies,)),
            pltpu.SemaphoreType.DMA((freqs,)),
            pltpu.SemaphoreType.DMA((freqs,)),
            pltpu.SemaphoreType.DMA((4,)),
            pltpu.SemaphoreType.REGULAR((6,)),
        ],
        compiler_params=pltpu.CompilerParams(
            collective_id=0, has_side_effects=True, vmem_limit_bytes=60 * 2**20
        ),
        name="gather_multiply_exchange",
    )(
        block_of_slot,
        receiver_order.reshape(1, rows),
        receivers.reshape(2 * rows, depth),
        data.reshape(2, slots, points // slots, width),
    )
    table = jnp.asarray(tables(freqs))
    each = width // (2 * freqs)
    groups = part // each
    traces = pl.pallas_call(
        transform_kernel,
        out_shape=jax.ShapeDtypeStruct((groups, each, width, NT), jnp.bfloat16),
        in_specs=[pl.BlockSpec(memory_space=pltpu.VMEM)] * 2,
        out_specs=pl.BlockSpec(memory_space=pl.ANY),
        scratch_shapes=[
            pltpu.VMEM((each, groups, width, NT), jnp.bfloat16),
            pltpu.SemaphoreType.DMA((each,)),
        ],
        name="transform",
    )(moved, table)
    return traces.reshape(part, width, NT)


def solution(mesh):
    placed = (P("freq", "src", None, None, None), P("freq", None, None, "src"), P(), P())
    return jax.shard_map(
        functools.partial(body, mesh.shape["freq"]),
        mesh=mesh,
        in_specs=placed,
        out_specs=P("freq", "src", None),
        check_vma=False,
    )
```

```python
import functools
import math

import jax
import jax.numpy as jnp
import numpy as np
from jax import lax
from jax.experimental import pallas as pl
from jax.experimental.pallas import tpu as pltpu
from jax.sharding import PartitionSpec as P

NT = 256
MESH = pl.DeviceIdType.MESH
CHUNK = 64


def sending_order(y_size, halves):
    def late(f):
        return 0.8 * (f // halves) + 2.2 * (f % halves)

    def need(f, q):
        dy = abs(f // halves - q // halves)
        hops = min(dy, y_size - dy) + 2 * (f % halves != q % halves)
        return 0.75 * hops + late(f) - late(q)

    count = y_size * halves
    return [sorted((q for q in range(count) if q != f), key=lambda q: -need(f, q)) + [f] for f in range(count)]


ORDER = sending_order(4, 2)

LOW, HIGH, EDGE = (0, 256), (256, 256), 80
AROUND = [(0, 1, EDGE, 2 * CHUNK - EDGE)] + [(0, 1, p * CHUNK, CHUNK) for p in range(2, 8)]
SENDS = {
    "xp": [(0, 0, *LOW), (0, 0, 256, 128)]
    + [(-1, 0, k * CHUNK, CHUNK) for k in range(4)]
    + [(0, 0, 384, 128)]
    + AROUND,
    "xm": [(0, 0, *LOW), (0, 0, *HIGH)]
    + AROUND[:2]
    + [(1, 0, k * CHUNK, CHUNK) for k in range(4, 8)]
    + AROUND[2:],
    "z": [(0, 0, *LOW), (0, 0, *HIGH), (-1, 0, 0, EDGE), (1, 0, 0, EDGE)]
    + [(2, 0, p * CHUNK, CHUNK) for p in range(8)],
    "c": [(0, 0, *LOW), (0, 0, *HIGH)]
    + [(-1, 0, *LOW), (1, 0, *LOW), (0, 1, *LOW)]
    + [(1, 0, *HIGH), (0, 1, *HIGH), (-1, 0, *HIGH)]
    + [(2, 0, *LOW), (2, 0, *HIGH)]
    + [(dx, 1, p * CHUNK, CHUNK) for p in range(8) for dx in (-1, 1, 2)],
}
SHIFT = {"xp": (-1, 0, 0), "xm": (1, 0, 0), "z": (0, 1, 0), "c": (0, 0, 1)}
COUNT = {link: len(rows) for link, rows in SENDS.items()}


def tables(count):
    times = np.arange(NT)
    bins = (2 * np.arange(count) + 1) * (NT // (4 * count))
    angle = (bins[:, None] * times[None, :] % NT) * (2.0 * math.pi / NT)
    full = np.stack([np.cos(angle), -np.sin(angle)], 1) * count ** (-0.5)
    full = full.reshape(2 * count, NT).astype(np.float32)
    high = full.astype(jnp.bfloat16).astype(np.float32)
    low = (full - high).astype(jnp.bfloat16).astype(np.float32)
    return np.concatenate([high, low], 0)


def gather_kernel(
    freqs, block_hbm, order_hbm, own_hbm, data_hbm, out_ref,
    block_ref, order_ref, held, data, raw, acc, perm, mix, outgoing, arrived,
    sx, rx, sf, rf, local, known,
):
    me = lax.axis_index("src")
    mine = lax.axis_index("freq")
    x, z, c = me // 4, (me // 2) % 2, me % 2
    depth = own_hbm.shape[1]
    rows = own_hbm.shape[0] // 2
    part = rows // freqs

    def slot(dx, dz, dc):
        return ((x + dx + 4) % 4) * 4 + ((z + dz) % 2) * 2 + (c + dc) % 2

    target = {"xp": slot(1, 0, 0), "xm": slot(-1, 0, 0), "z": slot(0, 1, 0), "c": slot(0, 0, 1)}
    first = {}
    at = 0
    for link in SENDS:
        first[link] = at
        at += COUNT[link]

    def place(p):
        if p == freqs - 1:
            return mine
        return sum(jnp.where(mine == f, ORDER[f][p], 0) for f in range(freqs))

    farther = {"xp": x < 3, "xm": x == 0, "z": z == 0, "c": c == 1}
    y, upper = mine // 2, mine % 2
    below = [(y == 0, 2 + upper), (y == 0, 6 + upper), (y == 1, 4 + upper), (mine == 0, 1)]
    above = jnp.where(y == 0, 0, jnp.where(y == 2, 2, 0) + upper)

    def one(flag):
        return jnp.where(flag, 1, 0)

    def greet(semaphore, peer):
        pl.semaphore_signal(semaphore, inc=1, device_id=peer, device_id_type=MESH)

    barrier = pltpu.get_barrier_semaphore()
    for link in SENDS:
        pl.when(farther[link])(functools.partial(greet, barrier, {"src": target[link]}))
    for flag, peer in below:
        pl.when(flag)(functools.partial(greet, barrier, {"freq": peer}))
    order_copy = pltpu.make_async_copy(order_hbm, order_ref, local.at[2])
    own_copy = pltpu.make_async_copy(own_hbm, raw, local.at[0])
    block_copy = pltpu.make_async_copy(block_hbm, block_ref, local.at[3])
    data_copy = pltpu.make_async_copy(data_hbm, data, local.at[1])
    for begun in (order_copy, own_copy, block_copy, data_copy):
        begun.start()
    nearer = sum(1 - one(farther[link]) for link in SENDS) + one(mine > 0)

    def enter():
        pl.semaphore_wait(barrier, nearer)

    pl.when(nearer > 0)(enter)
    for k, (link, far) in enumerate((("xp", "xm"), ("xm", "xp"), ("z", "z"), ("c", "c"))):
        pl.when(jnp.logical_not(farther[far]))(functools.partial(greet, known.at[k], {"src": target[far]}))

    peers_below = sum(one(flag) for flag, _ in below)

    def report():
        pl.when(peers_below > 0)(lambda: pl.semaphore_wait(known.at[4], peers_below))
        pl.when(mine > 0)(functools.partial(greet, known.at[4], {"freq": above}))

    def spread():
        pl.when(mine > 0)(lambda: pl.semaphore_wait(known.at[5], 1))
        for flag, peer in below:
            pl.when(flag)(functools.partial(greet, known.at[5], {"freq": peer}))

    def copy(link, k, received=False):
        dx, dz, low, count = SENDS[link][k]
        dc = 0
        if received:
            sx_, sz_, dc = SHIFT[link]
            dx, dz = dx + sx_, dz + sz_
        piece = held.at[slot(dx, dz, dc), pl.ds(low, count)]
        return pltpu.make_async_remote_copy(
            src_ref=piece,
            dst_ref=piece,
            send_sem=sx.at[first[link] + k],
            recv_sem=rx.at[first[link] + k],
            device_id={"src": target[link]},
            device_id_type=MESH,
        )

    def send(link, *which):
        for k in which:
            copy(link, k).start()

    def wait(link, *which):
        for k in which:
            copy(link, k, True).wait_recv()

    def product(blocks, low, count, arriving=(), fresh=False):
        span = pl.ds(low, count)
        value = 0.0 if fresh else acc[span, :]
        for n, (dx, dz, dc) in enumerate(blocks):
            if arriving:
                wait("c", arriving[n])
            j = slot(dx, dz, dc)
            block = block_ref[j]
            right = jnp.concatenate([data[0, block], data[1, block]], 1)
            value += jnp.dot(held[j, span, :], right, preferred_element_type=jnp.float32)
        acc[span, :] = value

    def finish(p):
        mid, half = p * CHUNK + part, acc.shape[1] // 2
        top, low = acc[p * CHUNK : mid, :], acc[mid : mid + part, :]
        real = top[:, :half] - low[:, half:]
        imag = top[:, half:] + low[:, :half]
        return jnp.concatenate([real, imag], 1).astype(jnp.bfloat16)

    def share(p, sender=mine):
        return pltpu.make_async_remote_copy(
            src_ref=outgoing.at[pl.ds(p * part, part)],
            dst_ref=arrived.at[pl.ds(pl.multiple_of(sender * part, part), part)],
            send_sem=sf.at[p],
            recv_sem=rf.at[sender],
            device_id={"freq": place(p)},
            device_id_type=MESH,
        )

    order_copy.wait()
    ids = lax.broadcasted_iota(jnp.int32, (rows, rows), 0)
    chosen = jnp.where(ids == order_ref[...], 1.0, 0.0).astype(jnp.float32)
    perm[...] = chosen.T.astype(jnp.bfloat16)
    own_copy.wait()
    for side in range(2):
        group = range(side * freqs // 2, (side + 1) * freqs // 2)
        picks = jnp.concatenate(
            [perm[pl.ds(pl.multiple_of(place(p) * part, part), part), :] for p in group], 0
        )
        for ri in range(2):
            wide = jnp.dot(picks, raw[ri * rows : (ri + 1) * rows, :], preferred_element_type=jnp.float32)
            for k, p in enumerate(group):
                held[me, pl.ds(p * CHUNK + ri * part, part), :] = wide[k * part : (k + 1) * part].astype(jnp.bfloat16)
    for near in (True, False):
        for k, link in enumerate(("xp", "xm", "z")):

            def begin(k=k, link=link, near=near):
                if not near:
                    pl.semaphore_wait(known.at[k], 1)
                send(link, 0, 1)

            pl.when(jnp.logical_not(farther[link]) if near else farther[link])(begin)
    pl.when(farther["c"])(lambda: pl.semaphore_wait(known.at[3], 1))
    send("c", 0, 1)

    n = lax.broadcasted_iota(jnp.int32, (2 * rows, 1), 0)
    source = (n % 2) * rows + ((n // 2) % freqs) * part + n // (2 * freqs)
    m = lax.broadcasted_iota(jnp.int32, (2 * rows, 2 * rows), 1)
    mix[...] = jnp.where(m == source, 1.0, 0.0).astype(jnp.bfloat16)

    block_copy.wait()
    data_copy.wait()
    product([(0, 0, 0)], 0, 2 * rows, fresh=True)

    wait("xp", 0)
    send("xp", 2, 3, 4, 5, 6)
    send("z", 2)
    wait("xm", 0)
    send("z", 3)
    wait("z", 0)
    send("xm", 2, 3)
    send("c", 2, 3, 4)
    wait("c", 0, 1)
    product([(0, 0, 1)], 0, 2 * rows)
    product([(-1, 0, 0), (1, 0, 0), (0, 1, 0)], *LOW)
    report()
    wait("c", 2, 3, 4)
    product([(-1, 0, 1), (1, 0, 1), (0, 1, 1)], *LOW)

    for k in range(2):
        wait("xp", 2 + k)
        send("z", 4 + k)
    wait("xm", 1)
    send("xm", 4, 5, 6, 7)
    wait("z", 1)
    send("xm", *range(8, 13))
    send("xp", *range(7, 14))
    send("c", 5, 6)
    product([(1, 0, 0), (0, 1, 0)], *HIGH)
    for k in range(2, 4):
        wait("xp", 2 + k)
        send("z", 4 + k)
    send("c", 8)
    wait("c", 5, 6)
    product([(1, 0, 1), (0, 1, 1)], *HIGH)
    product([(2, 0, 0)], *LOW)
    wait("xp", 1, 6)
    send("c", 7)
    product([(-1, 0, 0)], *HIGH)
    spread()
    for k in range(4):
        wait("xm", 4 + k)
        send("z", 8 + k)
    send("c", 9)
    product([(2, 0, 0)], *HIGH)
    wait("c", 7, 8, 9)
    product([(2, 0, 1)], *LOW)
    product([(-1, 0, 1), (2, 0, 1)], *HIGH)

    sides = (-1, 1, 2)
    here = pl.ds(pl.multiple_of(mine * part, part), part)
    for p in range(freqs + 1):
        if p < freqs:
            if p == 0:
                wait("z", 2, 3)
                send("c", 10, 11)
            wait("z", 4 + p)
            send("c", 12 + 3 * p)
            if p > 0:
                wait("xp", 6 + p)
                send("c", 10 + 3 * p)
                wait("xm", 1 + p if p < 3 else 5 + p)
                send("c", 11 + 3 * p)
            if p in (1, 3):
                product([(dx, 1, 0) for dx in sides], (p - 1) * CHUNK, 2 * CHUNK)
            elif p > 3:
                product([(dx, 1, 0) for dx in sides], p * CHUNK, CHUNK)
        if p > 0:
            last = p - 1
            if last in (0, 2):
                continue
            pair = last in (1, 3)
            if pair:
                wait("c", *range(7 + 3 * last, 10 + 3 * last))
            arrive = (2, 0, 1)
            product(
                [(sides[k], 1, 1) for k in arrive],
                (last - pair) * CHUNK,
                (1 + pair) * CHUNK,
                [10 + 3 * last + k for k in arrive],
            )
            if last == freqs - 1:
                arrived[here, :] = finish(last)
                continue
            for q in range(last - pair, last + 1):
                outgoing[pl.ds(q * part, part), :] = finish(q)
                share(q).start()
    for link in SENDS:
        for k in range(COUNT[link]):
            copy(link, k).wait_send()
    for p in range(freqs - 1):
        share(p, (mine + 1 + p) % freqs).wait_recv()

    half = acc.shape[1] // 2
    stacked = jnp.concatenate([arrived[:, :half], arrived[:, half:]], 0)
    mixed = jnp.dot(mix[...], stacked, preferred_element_type=jnp.float32)
    for g in range(2 * rows // half):
        span = pl.ds(g * half, half)
        out_ref[span, :] = mixed[g * half : (g + 1) * half, :].T.astype(jnp.bfloat16)
    for p in range(freqs - 1):
        share(p).wait_send()


def transform_kernel(spectra_ref, table_ref, out_hbm, done, sems):
    coefs = table_ref.shape[0] // 2
    each, groups, width, times = done.shape
    high, low = table_ref[:coefs, :], table_ref[coefs:, :]
    full = jnp.concatenate([high] * each + [low] * each, 0)
    row = lax.broadcasted_iota(jnp.int32, full.shape, 0)
    left = jnp.concatenate([spectra_ref[...], spectra_ref[...]], 1)
    copies = []
    for u in range(each):
        here = (row // coefs) % each == u
        right = jnp.where(here, full, 0.0).astype(jnp.bfloat16)
        value = jnp.dot(left, right, preferred_element_type=jnp.float32)
        done[u] = value.astype(jnp.bfloat16).reshape(groups, width, times)
        copies.append(pltpu.make_async_copy(done.at[u], out_hbm.at[:, u], sems.at[u]))
        copies[-1].start()
    for one in copies:
        one.wait()


def body(freqs, receivers, data, block_of_slot, receiver_order):
    rows, depth = receivers.shape[3], receivers.shape[4]
    points, width = data.shape[2], data.shape[3]
    slots = block_of_slot.shape[0]
    part = rows // freqs
    copies = sum(COUNT.values())
    moved = pl.pallas_call(
        functools.partial(gather_kernel, freqs),
        out_shape=jax.ShapeDtypeStruct((2 * rows, width), jnp.bfloat16),
        in_specs=[
            pl.BlockSpec(memory_space=pl.ANY),
            pl.BlockSpec(memory_space=pl.ANY),
            pl.BlockSpec(memory_space=pl.ANY),
            pl.BlockSpec(memory_space=pl.ANY),
        ],
        out_specs=pl.BlockSpec(memory_space=pltpu.VMEM),
        scratch_shapes=[
            pltpu.SMEM((slots,), jnp.int32),
            pltpu.VMEM((1, rows), jnp.int32),
            pltpu.VMEM((slots, 2 * rows, depth), jnp.bfloat16),
            pltpu.VMEM((2, slots, depth, width), jnp.bfloat16),
            pltpu.VMEM((2 * rows, depth), jnp.bfloat16),
            pltpu.VMEM((2 * rows, 2 * width), jnp.float32),
            pltpu.VMEM((rows, rows), jnp.bfloat16),
            pltpu.VMEM((2 * rows, 2 * rows), jnp.bfloat16),
            pltpu.VMEM((rows, 2 * width), jnp.bfloat16),
            pltpu.VMEM((rows, 2 * width), jnp.bfloat16),
            pltpu.SemaphoreType.DMA((copies,)),
            pltpu.SemaphoreType.DMA((copies,)),
            pltpu.SemaphoreType.DMA((freqs,)),
            pltpu.SemaphoreType.DMA((freqs,)),
            pltpu.SemaphoreType.DMA((4,)),
            pltpu.SemaphoreType.REGULAR((6,)),
        ],
        compiler_params=pltpu.CompilerParams(
            collective_id=0, has_side_effects=True, vmem_limit_bytes=60 * 2**20
        ),
        name="gather_multiply_exchange",
    )(
        block_of_slot,
        receiver_order.reshape(1, rows),
        receivers.reshape(2 * rows, depth),
        data.reshape(2, slots, points // slots, width),
    )
    table = jnp.asarray(tables(freqs))
    each = width // (2 * freqs)
    groups = part // each
    traces = pl.pallas_call(
        transform_kernel,
        out_shape=jax.ShapeDtypeStruct((groups, each, width, NT), jnp.bfloat16),
        in_specs=[pl.BlockSpec(memory_space=pltpu.VMEM)] * 2,
        out_specs=pl.BlockSpec(memory_space=pl.ANY),
        scratch_shapes=[
            pltpu.VMEM((each, groups, width, NT), jnp.bfloat16),
            pltpu.SemaphoreType.DMA((each,)),
        ],
        name="transform",
    )(moved, table)
    return traces.reshape(part, width, NT)


def solution(mesh):
    placed = (P("freq", "src", None, None, None), P("freq", None, None, "src"), P(), P())
    return jax.shard_map(
        functools.partial(body, mesh.shape["freq"]),
        mesh=mesh,
        in_specs=placed,
        out_specs=P("freq", "src", None),
        check_vma=False,
    )
```

```python
import functools
import math

import jax
import jax.numpy as jnp
import numpy as np
from jax import lax
from jax.experimental import pallas as pl
from jax.experimental.pallas import tpu as pltpu
from jax.sharding import PartitionSpec as P

NT = 256
MESH = pl.DeviceIdType.MESH
CHUNK = 64


def sending_order(y_size, halves):
    def late(f):
        return 0.4 * (f // halves) + 1.1 * (f % halves)

    def need(f, q):
        dy = abs(f // halves - q // halves)
        hops = min(dy, y_size - dy) + 2 * (f % halves != q % halves)
        return 0.75 * hops + late(f) - late(q)

    count = y_size * halves
    return [sorted((q for q in range(count) if q != f), key=lambda q: -need(f, q)) + [f] for f in range(count)]


ORDER = sending_order(4, 2)

LOW, HIGH, EDGE = (0, 256), (256, 256), 80
AROUND = [(0, 1, EDGE, 2 * CHUNK - EDGE)] + [(0, 1, p * CHUNK, CHUNK) for p in range(2, 8)]
SENDS = {
    "xp": [(0, 0, *LOW), (0, 0, 256, 128)]
    + [(-1, 0, k * CHUNK, CHUNK) for k in range(4)]
    + [(0, 0, 384, 128)]
    + AROUND,
    "xm": [(0, 0, *LOW), (0, 0, *HIGH)]
    + AROUND[:2]
    + [(1, 0, k * CHUNK, CHUNK) for k in range(4, 8)]
    + AROUND[2:],
    "z": [(0, 0, *LOW), (0, 0, *HIGH), (-1, 0, 0, EDGE), (1, 0, 0, EDGE)]
    + [(2, 0, p * CHUNK, CHUNK) for p in range(8)],
    "c": [(0, 0, *LOW), (0, 0, *HIGH)]
    + [(-1, 0, *LOW), (1, 0, *LOW), (0, 1, *LOW)]
    + [(1, 0, *HIGH), (0, 1, *HIGH), (-1, 0, *HIGH)]
    + [(2, 0, *LOW), (2, 0, *HIGH)]
    + [(dx, 1, p * CHUNK, CHUNK) for p in range(8) for dx in (-1, 1, 2)],
}
SHIFT = {"xp": (-1, 0, 0), "xm": (1, 0, 0), "z": (0, 1, 0), "c": (0, 0, 1)}
COUNT = {link: len(rows) for link, rows in SENDS.items()}


def tables(count):
    times = np.arange(NT)
    bins = (2 * np.arange(count) + 1) * (NT // (4 * count))
    angle = (bins[:, None] * times[None, :] % NT) * (2.0 * math.pi / NT)
    full = np.stack([np.cos(angle), -np.sin(angle)], 1) * count ** (-0.5)
    full = full.reshape(2 * count, NT).astype(np.float32)
    high = full.astype(jnp.bfloat16).astype(np.float32)
    low = (full - high).astype(jnp.bfloat16).astype(np.float32)
    return np.concatenate([high, low], 0)


def gather_kernel(
    freqs, block_hbm, order_hbm, own_hbm, data_hbm, out_ref,
    block_ref, order_ref, held, data, raw, acc, perm, mix, outgoing, arrived,
    sx, rx, sf, rf, local, known,
):
    me = lax.axis_index("src")
    mine = lax.axis_index("freq")
    x, z, c = me // 4, (me // 2) % 2, me % 2
    depth = own_hbm.shape[1]
    rows = own_hbm.shape[0] // 2
    part = rows // freqs

    def slot(dx, dz, dc):
        return ((x + dx + 4) % 4) * 4 + ((z + dz) % 2) * 2 + (c + dc) % 2

    target = {"xp": slot(1, 0, 0), "xm": slot(-1, 0, 0), "z": slot(0, 1, 0), "c": slot(0, 0, 1)}
    first = {}
    at = 0
    for link in SENDS:
        first[link] = at
        at += COUNT[link]

    def place(p):
        if p == freqs - 1:
            return mine
        return sum(jnp.where(mine == f, ORDER[f][p], 0) for f in range(freqs))

    farther = {"xp": x < 3, "xm": x == 0, "z": z == 0, "c": c == 1}
    y, upper = mine // 2, mine % 2
    below = [(y == 0, 2 + upper), (y == 0, 6 + upper), (y == 1, 4 + upper), (mine == 0, 1)]
    above = jnp.where(y == 0, 0, jnp.where(y == 2, 2, 0) + upper)

    def one(flag):
        return jnp.where(flag, 1, 0)

    def greet(semaphore, peer):
        pl.semaphore_signal(semaphore, inc=1, device_id=peer, device_id_type=MESH)

    barrier = pltpu.get_barrier_semaphore()
    for link in SENDS:
        pl.when(farther[link])(functools.partial(greet, barrier, {"src": target[link]}))
    for flag, peer in below:
        pl.when(flag)(functools.partial(greet, barrier, {"freq": peer}))
    order_copy = pltpu.make_async_copy(order_hbm, order_ref, local.at[2])
    own_copy = pltpu.make_async_copy(own_hbm, raw, local.at[0])
    block_copy = pltpu.make_async_copy(block_hbm, block_ref, local.at[3])
    data_copy = pltpu.make_async_copy(data_hbm, data, local.at[1])
    for begun in (order_copy, own_copy, block_copy, data_copy):
        begun.start()
    nearer = sum(1 - one(farther[link]) for link in SENDS) + one(mine > 0)

    def enter():
        pl.semaphore_wait(barrier, nearer)

    pl.when(nearer > 0)(enter)
    for k, (link, far) in enumerate((("xp", "xm"), ("xm", "xp"), ("z", "z"), ("c", "c"))):
        pl.when(jnp.logical_not(farther[far]))(functools.partial(greet, known.at[k], {"src": target[far]}))

    peers_below = sum(one(flag) for flag, _ in below)

    def report():
        pl.when(peers_below > 0)(lambda: pl.semaphore_wait(known.at[4], peers_below))
        pl.when(mine > 0)(functools.partial(greet, known.at[4], {"freq": above}))

    def spread():
        pl.when(mine > 0)(lambda: pl.semaphore_wait(known.at[5], 1))
        for flag, peer in below:
            pl.when(flag)(functools.partial(greet, known.at[5], {"freq": peer}))

    def copy(link, k, received=False):
        dx, dz, low, count = SENDS[link][k]
        dc = 0
        if received:
            sx_, sz_, dc = SHIFT[link]
            dx, dz = dx + sx_, dz + sz_
        piece = held.at[slot(dx, dz, dc), pl.ds(low, count)]
        return pltpu.make_async_remote_copy(
            src_ref=piece,
            dst_ref=piece,
            send_sem=sx.at[first[link] + k],
            recv_sem=rx.at[first[link] + k],
            device_id={"src": target[link]},
            device_id_type=MESH,
        )

    def send(link, *which):
        for k in which:
            copy(link, k).start()

    def wait(link, *which):
        for k in which:
            copy(link, k, True).wait_recv()

    def product(blocks, low, count, arriving=(), fresh=False):
        span = pl.ds(low, count)
        value = 0.0 if fresh else acc[span, :]
        for n, (dx, dz, dc) in enumerate(blocks):
            if arriving:
                wait("c", arriving[n])
            j = slot(dx, dz, dc)
            block = block_ref[j]
            right = jnp.concatenate([data[0, block], data[1, block]], 1)
            value += jnp.dot(held[j, span, :], right, preferred_element_type=jnp.float32)
        acc[span, :] = value

    def finish(p):
        mid, half = p * CHUNK + part, acc.shape[1] // 2
        top, low = acc[p * CHUNK : mid, :], acc[mid : mid + part, :]
        real = top[:, :half] - low[:, half:]
        imag = top[:, half:] + low[:, :half]
        return jnp.concatenate([real, imag], 1).astype(jnp.bfloat16)

    def share(p, sender=mine):
        return pltpu.make_async_remote_copy(
            src_ref=outgoing.at[pl.ds(p * part, part)],
            dst_ref=arrived.at[pl.ds(pl.multiple_of(sender * part, part), part)],
            send_sem=sf.at[p],
            recv_sem=rf.at[sender],
            device_id={"freq": place(p)},
            device_id_type=MESH,
        )

    order_copy.wait()
    ids = lax.broadcasted_iota(jnp.int32, (rows, rows), 0)
    chosen = jnp.where(ids == order_ref[...], 1.0, 0.0).astype(jnp.float32)
    perm[...] = chosen.T.astype(jnp.bfloat16)
    own_copy.wait()
    for side in range(2):
        group = range(side * freqs // 2, (side + 1) * freqs // 2)
        picks = jnp.concatenate(
            [perm[pl.ds(pl.multiple_of(place(p) * part, part), part), :] for p in group], 0
        )
        for ri in range(2):
            wide = jnp.dot(picks, raw[ri * rows : (ri + 1) * rows, :], preferred_element_type=jnp.float32)
            for k, p in enumerate(group):
                held[me, pl.ds(p * CHUNK + ri * part, part), :] = wide[k * part : (k + 1) * part].astype(jnp.bfloat16)
    for near in (True, False):
        for k, link in enumerate(("xp", "xm", "z")):

            def begin(k=k, link=link, near=near):
                if not near:
                    pl.semaphore_wait(known.at[k], 1)
                send(link, 0, 1)

            pl.when(jnp.logical_not(farther[link]) if near else farther[link])(begin)
    pl.when(farther["c"])(lambda: pl.semaphore_wait(known.at[3], 1))
    send("c", 0, 1)

    n = lax.broadcasted_iota(jnp.int32, (2 * rows, 1), 0)
    source = (n % 2) * rows + ((n // 2) % freqs) * part + n // (2 * freqs)
    m = lax.broadcasted_iota(jnp.int32, (2 * rows, 2 * rows), 1)
    mix[...] = jnp.where(m == source, 1.0, 0.0).astype(jnp.bfloat16)

    block_copy.wait()
    data_copy.wait()
    product([(0, 0, 0)], 0, 2 * rows, fresh=True)

    wait("xp", 0)
    send("xp", 2, 3, 4, 5, 6)
    send("z", 2)
    wait("xm", 0)
    send("z", 3)
    wait("z", 0)
    send("xm", 2, 3)
    send("c", 2, 3, 4)
    wait("c", 0, 1)
    product([(0, 0, 1)], 0, 2 * rows)
    product([(-1, 0, 0), (1, 0, 0), (0, 1, 0)], *LOW)
    report()
    wait("c", 2, 3, 4)
    product([(-1, 0, 1), (1, 0, 1), (0, 1, 1)], *LOW)

    for k in range(2):
        wait("xp", 2 + k)
        send("z", 4 + k)
    wait("xm", 1)
    send("xm", 4, 5, 6, 7)
    wait("z", 1)
    send("xm", *range(8, 13))
    send("xp", *range(7, 14))
    send("c", 5, 6)
    product([(1, 0, 0), (0, 1, 0)], *HIGH)
    for k in range(2, 4):
        wait("xp", 2 + k)
        send("z", 4 + k)
    send("c", 8)
    wait("c", 5, 6)
    product([(1, 0, 1), (0, 1, 1)], *HIGH)
    product([(2, 0, 0)], *LOW)
    wait("xp", 1, 6)
    send("c", 7)
    product([(-1, 0, 0)], *HIGH)
    spread()
    for k in range(4):
        wait("xm", 4 + k)
        send("z", 8 + k)
    send("c", 9)
    product([(2, 0, 0)], *HIGH)
    wait("c", 7, 8, 9)
    product([(2, 0, 1)], *LOW)
    product([(-1, 0, 1), (2, 0, 1)], *HIGH)

    sides = (-1, 1, 2)
    here = pl.ds(pl.multiple_of(mine * part, part), part)
    for p in range(freqs + 1):
        if p < freqs:
            if p == 0:
                wait("z", 2, 3)
                send("c", 10, 11)
            wait("z", 4 + p)
            send("c", 12 + 3 * p)
            if p > 0:
                wait("xp", 6 + p)
                send("c", 10 + 3 * p)
                wait("xm", 1 + p if p < 3 else 5 + p)
                send("c", 11 + 3 * p)
            if p in (1, 3):
                product([(dx, 1, 0) for dx in sides], (p - 1) * CHUNK, 2 * CHUNK)
            elif p > 3:
                product([(dx, 1, 0) for dx in sides], p * CHUNK, CHUNK)
        if p > 0:
            last = p - 1
            if last in (0, 2):
                continue
            pair = last in (1, 3)
            if pair:
                wait("c", *range(7 + 3 * last, 10 + 3 * last))
            arrive = (2, 0, 1)
            product(
                [(sides[k], 1, 1) for k in arrive],
                (last - pair) * CHUNK,
                (1 + pair) * CHUNK,
                [10 + 3 * last + k for k in arrive],
            )
            if last == freqs - 1:
                arrived[here, :] = finish(last)
                continue
            for q in range(last - pair, last + 1):
                outgoing[pl.ds(q * part, part), :] = finish(q)
                share(q).start()
    for link in SENDS:
        for k in range(COUNT[link]):
            copy(link, k).wait_send()
    for p in range(freqs - 1):
        share(p, (mine + 1 + p) % freqs).wait_recv()

    half = acc.shape[1] // 2
    stacked = jnp.concatenate([arrived[:, :half], arrived[:, half:]], 0)
    mixed = jnp.dot(mix[...], stacked, preferred_element_type=jnp.float32)
    for g in range(2 * rows // half):
        span = pl.ds(g * half, half)
        out_ref[span, :] = mixed[g * half : (g + 1) * half, :].T.astype(jnp.bfloat16)
    for p in range(freqs - 1):
        share(p).wait_send()


def transform_kernel(spectra_ref, table_ref, out_hbm, done, sems):
    coefs = table_ref.shape[0] // 2
    each, groups, width, times = done.shape
    high, low = table_ref[:coefs, :], table_ref[coefs:, :]
    full = jnp.concatenate([high] * each + [low] * each, 0)
    row = lax.broadcasted_iota(jnp.int32, full.shape, 0)
    left = jnp.concatenate([spectra_ref[...], spectra_ref[...]], 1)
    copies = []
    for u in range(each):
        here = (row // coefs) % each == u
        right = jnp.where(here, full, 0.0).astype(jnp.bfloat16)
        value = jnp.dot(left, right, preferred_element_type=jnp.float32)
        done[u] = value.astype(jnp.bfloat16).reshape(groups, width, times)
        copies.append(pltpu.make_async_copy(done.at[u], out_hbm.at[:, u], sems.at[u]))
        copies[-1].start()
    for one in copies:
        one.wait()


def body(freqs, receivers, data, block_of_slot, receiver_order):
    rows, depth = receivers.shape[3], receivers.shape[4]
    points, width = data.shape[2], data.shape[3]
    slots = block_of_slot.shape[0]
    part = rows // freqs
    copies = sum(COUNT.values())
    moved = pl.pallas_call(
        functools.partial(gather_kernel, freqs),
        out_shape=jax.ShapeDtypeStruct((2 * rows, width), jnp.bfloat16),
        in_specs=[
            pl.BlockSpec(memory_space=pl.ANY),
            pl.BlockSpec(memory_space=pl.ANY),
            pl.BlockSpec(memory_space=pl.ANY),
            pl.BlockSpec(memory_space=pl.ANY),
        ],
        out_specs=pl.BlockSpec(memory_space=pltpu.VMEM),
        scratch_shapes=[
            pltpu.SMEM((slots,), jnp.int32),
            pltpu.VMEM((1, rows), jnp.int32),
            pltpu.VMEM((slots, 2 * rows, depth), jnp.bfloat16),
            pltpu.VMEM((2, slots, depth, width), jnp.bfloat16),
            pltpu.VMEM((2 * rows, depth), jnp.bfloat16),
            pltpu.VMEM((2 * rows, 2 * width), jnp.float32),
            pltpu.VMEM((rows, rows), jnp.bfloat16),
            pltpu.VMEM((2 * rows, 2 * rows), jnp.bfloat16),
            pltpu.VMEM((rows, 2 * width), jnp.bfloat16),
            pltpu.VMEM((rows, 2 * width), jnp.bfloat16),
            pltpu.SemaphoreType.DMA((copies,)),
            pltpu.SemaphoreType.DMA((copies,)),
            pltpu.SemaphoreType.DMA((freqs,)),
            pltpu.SemaphoreType.DMA((freqs,)),
            pltpu.SemaphoreType.DMA((4,)),
            pltpu.SemaphoreType.REGULAR((6,)),
        ],
        compiler_params=pltpu.CompilerParams(
            collective_id=0, has_side_effects=True, vmem_limit_bytes=60 * 2**20
        ),
        name="gather_multiply_exchange",
    )(
        block_of_slot,
        receiver_order.reshape(1, rows),
        receivers.reshape(2 * rows, depth),
        data.reshape(2, slots, points // slots, width),
    )
    table = jnp.asarray(tables(freqs))
    each = width // (2 * freqs)
    groups = part // each
    traces = pl.pallas_call(
        transform_kernel,
        out_shape=jax.ShapeDtypeStruct((groups, each, width, NT), jnp.bfloat16),
        in_specs=[pl.BlockSpec(memory_space=pltpu.VMEM)] * 2,
        out_specs=pl.BlockSpec(memory_space=pl.ANY),
        scratch_shapes=[
            pltpu.VMEM((each, groups, width, NT), jnp.bfloat16),
            pltpu.SemaphoreType.DMA((each,)),
        ],
        name="transform",
    )(moved, table)
    return traces.reshape(part, width, NT)


def solution(mesh):
    placed = (P("freq", "src", None, None, None), P("freq", None, None, "src"), P(), P())
    return jax.shard_map(
        functools.partial(body, mesh.shape["freq"]),
        mesh=mesh,
        in_specs=placed,
        out_specs=P("freq", "src", None),
        check_vma=False,
    )
```
